32 devices in a mesh: ids: 8 (over z, x), mdl: 4 (over y, core).
Axes of the slice: x: 2, y: 2, z: 4, core: 2. Of those that a mesh axis runs over, the one named last changes fastest.
Arguments:
- hash_codes: int32 [32768, 1024], P('ids', 'mdl'), may hold values from 0 to 1023
- request_ids: int32 [64, 1024], P('ids'), may hold values from 0 to 32767, as said below
- request_counts: int32 [64], P('ids'), may hold values from 256 to 1024, as said below
- token_slots: int32 [65536], P('ids'), may hold values from 0 to 8191, as said below
- cotangent: bfloat16 [65536, 32], P('ids'), may hold values from -6 to 6
- weight_first: float32 [1024, 1800], P('ids', 'mdl'), may hold values from -0.1875 to 0.1875
- weight_second: float32 [1800, 1800], P(None, 'mdl'), may hold values from -0.125 to 0.125
- weight_final: float32 [1800, 32], P('mdl'), may hold values from -0.125 to 0.125
- norm_params: float32 [4, 1800], P(None, 'mdl')
- bias_final: float32 [32], replicated, may hold values from -0.5 to 0.5
- moment_first: float32 [1024, 1800], P('ids', 'mdl'), may hold values from -0.0007324219 to 0.0007324219
- square_first: float32 [1024, 1800], P('ids', 'mdl'), may hold values from 1.373291e-09 to 5.493164e-09
- moment_second: float32 [1800, 1800], P(None, 'mdl'), may hold values from -0.0007324219 to 0.0007324219
- square_second: float32 [1800, 1800], P(None, 'mdl'), may hold values from 1.373291e-09 to 5.493164e-09
- moment_final: float32 [1800, 32], P('mdl'), may hold values from -0.0048828125 to 0.0048828125
- square_final: float32 [1800, 32], P('mdl'), may hold values from 6.103516e-08 to 2.4414064e-07
- moment_norm: float32 [4, 1800], P(None, 'mdl'), may hold values from -0.001953125 to 0.001953125
- square_norm: float32 [4, 1800], P(None, 'mdl'), may hold values from 9e-09 to 3.6e-08
- moment_bias: float32 [32], replicated, may hold values from -0.03125 to 0.03125
- square_bias: float32 [32], replicated, may hold values from 2.5e-06 to 1e-05
Outputs:
- token_embed: bfloat16 [65536, 32], P('ids')
- momentum_first: float32 [1024, 1800], P('ids', 'mdl')
- variance_first: float32 [1024, 1800], P('ids', 'mdl')
- master_first: float32 [1024, 1800], P('ids', 'mdl')
- bfloat_first: bfloat16 [1024, 1800], P('ids', 'mdl')
- momentum_second: float32 [1800, 1800], P(None, 'mdl')
- variance_second: float32 [1800, 1800], P(None, 'mdl')
- master_second: float32 [1800, 1800], P(None, 'mdl')
- bfloat_second: bfloat16 [1800, 1800], P(None, 'mdl')
- momentum_final: float32 [1800, 32], P('mdl')
- variance_final: float32 [1800, 32], P('mdl')
- master_final: float32 [1800, 32], P('mdl')
- bfloat_final: bfloat16 [1800, 32], P('mdl')
- momentum_norm: float32 [4, 1800], P(None, 'mdl')
- variance_norm: float32 [4, 1800], P(None, 'mdl')
- master_norm: float32 [4, 1800], P(None, 'mdl')
- momentum_bias: float32 [32], replicated
- variance_bias: float32 [32], replicated
- master_bias: float32 [32], replicated
The draws below stay inside these ranges and needn't reach their ends.
Inputs may be any that keep to these rules, and one draw needn't show every extreme that they name: `request_ids`: entries of row s * 8 + j lie in owner j's range j * 4096 to (j + 1) * 4096 - 1; the live ones (the first request_counts of the row) are distinct; the others are padding. `request_counts`: some owner receives exactly 1024 live ids from every device. `token_slots`: each token points at a live slot of its own device, and every live slot of a device is pointed at by one or more of its tokens.
All inputs are finite; a program needn't handle non-finite values.
Results may differ from the reference program's by a relative error of at most 0.003.
The reference program's roundings to bfloat16 on the way count: a program that leaves them out, or rounds other values in their place, can miss the bound.
Values may be sent and summed in bfloat16 or wider, within the bound.
A program may use at most 256 MiB of HBM per device.

```python
import math
import jax
import jax.numpy as jnp
from jax import lax

IN_DIM = 1024
HID = 1800
OUT_DIM = 32
R_DEV = 4096
TOK_DEV = 8192
STEP = 10
OWNERS = 8
CAP = 1024
TOKENS = 65536
ID_RANGE = 32768


def pin_value(perm, slot, value):
    current = perm[slot]
    perm = jnp.where(perm == value, current, perm)
    return perm.at[slot].set(value)


def request_plan(key):
    base_key = jax.random.fold_in(key, 7)
    key_list = jax.random.split(base_key, 7)
    source_grid = jnp.arange(OWNERS, dtype=jnp.int32)[:, None]
    owner_row = jnp.arange(OWNERS, dtype=jnp.int32)[None, :]
    counts = jax.random.randint(key_list[0], (OWNERS, OWNERS), CAP // 4, CAP + 1, dtype=jnp.int32)
    full_owner = jax.random.randint(key_list[1], (), 0, OWNERS, dtype=jnp.int32)
    forced = (owner_row == full_owner) | (source_grid == 0) & (owner_row == OWNERS - 1)
    counts = jnp.where(forced, CAP, counts)
    forced_low = (source_grid == OWNERS - 1) & (owner_row == (full_owner + 1) % OWNERS)
    counts = jnp.where(forced_low, CAP // 4, counts)
    pool_size = jnp.maximum(CAP, R_DEV * (1 + 7 * owner_row // max(OWNERS - 1, 1)) // 8)
    orders = jax.vmap(lambda member: jax.random.permutation(jax.random.fold_in(key_list[2], member), R_DEV))(jnp.arange(OWNERS))
    orders = orders.astype(jnp.int32)
    offset = jax.random.randint(key_list[3], (OWNERS, OWNERS), 0, jnp.broadcast_to(pool_size, (OWNERS, OWNERS)), dtype=jnp.int32)
    position = jnp.arange(CAP, dtype=jnp.int32)
    inside = (offset[:, :, None] + position[None, None, :]) % pool_size[:, :, None]
    padding = jax.random.randint(key_list[4], (OWNERS, OWNERS, CAP), 0, R_DEV, dtype=jnp.int32)
    used_slot = position[None, None, :] < counts[:, :, None]
    local_row = jnp.where(used_slot, inside, padding)
    orders = orders.at[0].set(pin_value(orders[0], local_row[0, 0, 0], 0))
    orders = orders.at[OWNERS - 1].set(pin_value(orders[OWNERS - 1], local_row[0, OWNERS - 1, 0], R_DEV - 1))
    owner_grid = jnp.broadcast_to(owner_row[:, :, None], local_row.shape)
    id_values = owner_grid * R_DEV + orders[owner_grid, local_row]
    flat_used = used_slot.reshape(OWNERS, OWNERS * CAP)
    slot_order = jnp.argsort(jnp.where(flat_used, 0, 1), axis=1, stable=True).astype(jnp.int32)
    uniques = jnp.sum(counts, axis=1)
    token_index = jnp.arange(TOK_DEV, dtype=jnp.int32)[None, :]
    extra_pick = jax.random.randint(key_list[5], (OWNERS, TOK_DEV), 0, uniques[:, None], dtype=jnp.int32)
    chosen = jnp.where(token_index < uniques[:, None], token_index, extra_pick)
    slot_list = jnp.take_along_axis(slot_order, chosen, axis=1)
    shuffle = jax.vmap(lambda member: jax.random.permutation(jax.random.fold_in(key_list[6], member), TOK_DEV))(jnp.arange(OWNERS))
    slot_list = jnp.take_along_axis(slot_list, shuffle.astype(jnp.int32), axis=1)
    return (id_values.reshape(OWNERS * OWNERS, CAP).astype(jnp.int32), counts.reshape(OWNERS * OWNERS).astype(jnp.int32), slot_list.reshape(OWNERS * TOK_DEV).astype(jnp.int32))


def draw_request_ids(key, part):
    return request_plan(key)[0]


def draw_request_counts(key, part):
    return request_plan(key)[1]


def draw_token_slots(key, part):
    return request_plan(key)[2]


def draw_norm_params(key, part):
    gain_key, shift_key = jax.random.split(jax.random.fold_in(key, 11))
    gain_rows = 1.0 + 0.15 * jnp.clip(jax.random.normal(gain_key, (2, HID)), -3.0, 3.0)
    shift_rows = 0.3 * jnp.clip(jax.random.normal(shift_key, (2, HID)), -4.0, 4.0)
    return jnp.stack([gain_rows[0], shift_rows[0], gain_rows[1], shift_rows[1]]).astype(jnp.float32)


def set_ends(drawn, key, low, high):
    place = [jax.random.randint(jax.random.fold_in(key, axis), (), 0, length) for axis, length in enumerate(drawn.shape)]
    main_axis = drawn.shape.index(max(drawn.shape))
    neighbour = place[:main_axis] + [(place[main_axis] + 1) % drawn.shape[main_axis]] + place[main_axis + 1:]
    return drawn.at[tuple(place)].set(low).at[tuple(neighbour)].set(high)


def block_levels(rng, extent, cuts, smallest, largest):
    def one(dim, blocks):
        draws = jax.random.uniform(jax.random.fold_in(jax.random.fold_in(rng, 6), dim), (blocks,), jnp.float32, smallest / len(cuts), largest / len(cuts))
        return jnp.repeat(jnp.exp(draws), extent[dim] // blocks).reshape((-1,) + (1,) * (len(extent) - dim - 1))

    level = one(*cuts[0])
    for cut in cuts[1:]:
        level = level * one(*cut)
    return level


def noise(key, shape, deviation, bound, pieces=(), held_as=jnp.bfloat16):
    values = jax.random.normal(key, shape, jnp.float32) * deviation
    if len(pieces) > 0:
        values = block_levels(key, shape, pieces, -0.22, 0.18) * values
    return jnp.clip(values, min=-bound, max=bound).astype(held_as)


def setup_inputs(seed: int = 0) -> dict:
    seeds = jax.random.split(jax.random.key(seed), 21)
    hash_codes = set_ends(jax.random.randint(seeds[0], (ID_RANGE, IN_DIM), 0, 1024), jax.random.fold_in(seeds[0], 1), 0, 1023).astype(jnp.int32)
    request_ids = draw_request_ids(jax.random.fold_in(seeds[20], 71), 0)
    request_counts = draw_request_counts(jax.random.fold_in(seeds[20], 71), 0)
    token_slots = draw_token_slots(jax.random.fold_in(seeds[20], 71), 0)
    cotangent = noise(seeds[4], (TOKENS, OUT_DIM), 1.0, 6.0, ((0, 8),))
    weight_first = noise(seeds[5], (IN_DIM, HID), IN_DIM ** -0.5, 0.1875, ((0, 8), (1, 4)), jnp.float32)
    weight_second = noise(seeds[6], (HID, HID), HID ** -0.5, 0.125, ((1, 4),), jnp.float32)
    weight_final = noise(seeds[7], (HID, OUT_DIM), HID ** -0.5, 0.125, ((0, 4),), jnp.float32)
    norm_params = draw_norm_params(jax.random.fold_in(seeds[20], 71), 0)
    bias_final = noise(seeds[9], (OUT_DIM,), 0.1, 0.5, (), jnp.float32)
    moment_first = noise(seeds[10], (IN_DIM, HID), (0.033 * TOKENS ** -0.5), 0.0007324219, ((0, 8), (1, 4)), jnp.float32)
    square_first = jnp.clip(jnp.exp(math.log(5.493164145775609e-09) - 1.3862944 * jax.random.uniform(seeds[11], (IN_DIM, HID), jnp.float32) ** block_levels(seeds[11], (IN_DIM, HID), ((0, 8), (1, 4)), -0.2, 0.2)), 1.3732910364439022e-09, 5.493164145775609e-09)
    moment_second = noise(seeds[12], (HID, HID), (0.033 * TOKENS ** -0.5), 0.0007324219, ((1, 4),), jnp.float32)
    square_second = jnp.clip(jnp.exp(math.log(5.493164145775609e-09) - 1.3862944 * jax.random.uniform(seeds[13], (HID, HID), jnp.float32) ** block_levels(seeds[13], (HID, HID), ((1, 4),), -0.2, 0.2)), 1.3732910364439022e-09, 5.493164145775609e-09)
    moment_final = noise(seeds[14], (HID, OUT_DIM), (0.22 * TOKENS ** -0.5), 0.0048828125, ((0, 4),), jnp.float32)
    square_final = jnp.clip(jnp.exp(math.log(2.4414063659605745e-07) - 1.3862944 * jax.random.uniform(seeds[15], (HID, OUT_DIM), jnp.float32) ** block_levels(seeds[15], (HID, OUT_DIM), ((0, 4),), -0.2, 0.2)), 6.103515914901436e-08, 2.4414063659605745e-07)
    moment_norm = noise(seeds[16], (4, HID), 0.00033, 0.001953125, ((1, 4),), jnp.float32)
    square_norm = jnp.clip(jnp.exp(math.log(3.599999942593968e-08) - 1.3862944 * jax.random.uniform(seeds[17], (4, HID), jnp.float32) ** block_levels(seeds[17], (4, HID), ((1, 4),), -0.2, 0.2)), 8.99999985648492e-09, 3.599999942593968e-08)
    moment_bias = noise(seeds[18], (OUT_DIM,), 0.0055, 0.03125, (), jnp.float32)
    square_bias = jnp.clip(jnp.exp(jax.random.uniform(seeds[19], (OUT_DIM,), jnp.float32, math.log(2.499999936844688e-06), math.log(9.999999747378752e-06))), 2.499999936844688e-06, 9.999999747378752e-06)
    return {"hash_codes": hash_codes, "request_ids": request_ids, "request_counts": request_counts, "token_slots": token_slots, "cotangent": cotangent, "weight_first": weight_first, "weight_second": weight_second, "weight_final": weight_final, "norm_params": norm_params, "bias_final": bias_final, "moment_first": moment_first, "square_first": square_first, "moment_second": moment_second, "square_second": square_second, "moment_final": moment_final, "square_final": square_final, "moment_norm": moment_norm, "square_norm": square_norm, "moment_bias": moment_bias, "square_bias": square_bias}


@jax.custom_vjp
def low(v):
    return lax.optimization_barrier(v.astype(jnp.bfloat16)).astype(jnp.float32)

@jax.custom_vjp
def low_back(v):
    return v

def low_keep(v):
    return (low(v), None)

def low_pass(kept, grad):
    return (grad,)

def back_keep(v):
    return (v, None)

def back_low(kept, grad):
    return (low(grad),)
low.defvjp(low_keep, low_pass)
low_back.defvjp(back_keep, back_low)
beta_one = 0.9
beta_two = 0.999
adam_epsilon = 1e-08
norm_epsilon = 1e-05
penalty_weight = 0.25
decay_matrix = 0.01
rate_matrix = 0.05
rate_norm = 0.5
rate_bias = 0.02

def mish(inputs):
    return inputs * jnp.tanh(jax.nn.softplus(inputs))

def adam(weight, moment, square, gradient, step_rate, shrink):
    momentum = beta_one * moment + (1.0 - beta_one) * gradient
    variance = beta_two * square + (1.0 - beta_two) * gradient * gradient
    moment_hat = momentum / (1.0 - beta_one ** STEP)
    square_hat = variance / (1.0 - beta_two ** STEP)
    master = weight - step_rate * (moment_hat / (jnp.sqrt(square_hat) + adam_epsilon) + shrink * weight)
    return (momentum, variance, master)

def reference(hash_codes, request_ids, request_counts, token_slots, cotangent, weight_first, weight_second, weight_final, norm_params, bias_final, moment_first, square_first, moment_second, square_second, moment_final, square_final, moment_norm, square_norm, moment_bias, square_bias):
    highest = lax.Precision.HIGHEST
    flat_ids = request_ids.reshape(-1)
    live_slot = (jnp.arange(CAP)[None, :] < request_counts[:, None]).astype(jnp.float32).reshape(-1)
    hit_count = jax.ops.segment_sum(live_slot, flat_ids, num_segments=ID_RANGE)
    live_mask = jnp.minimum(hit_count, 1.0)
    live_count = jnp.sum(live_mask)
    sources = jnp.arange(TOKENS) // TOK_DEV
    token_rows = flat_ids[sources * TOK_DEV + token_slots]
    signal = jax.ops.segment_sum(cotangent.astype(jnp.float32) / TOKENS, token_rows, num_segments=ID_RANGE)
    encoded = low((hash_codes.astype(jnp.float32) + 0.5) / 512.0 - 1.0)
    features = encoded.reshape(OWNERS, R_DEV, IN_DIM)
    live_blocks = live_mask.reshape(OWNERS, R_DEV, 1)
    signal_blocks = signal.reshape(OWNERS, R_DEV, OUT_DIM)

    def total(params):
        matrix_one, matrix_two, matrix_three, norm_rows, bias_row = params
        one_low = low(matrix_one)
        two_low = low(matrix_two)
        three_low = low(matrix_three)

        def layer_one(block_rows):
            return mish(low_back(jnp.dot(block_rows, one_low, precision=highest)))
        active_one = lax.map(jax.checkpoint(layer_one), features)
        mean_one = lax.optimization_barrier(jnp.sum(live_blocks * active_one, axis=(0, 1))) / live_count
        scale_one = lax.rsqrt(lax.optimization_barrier(jnp.sum(live_blocks * active_one * active_one, axis=(0, 1))) / live_count - mean_one * mean_one + norm_epsilon)

        def layer_two(block_rows):
            normed = low(norm_rows[0] * ((block_rows - mean_one) * scale_one) + norm_rows[1])
            return mish(low_back(jnp.dot(normed, two_low, precision=highest)))
        active_two = lax.map(jax.checkpoint(layer_two), active_one)
        mean_two = lax.optimization_barrier(jnp.sum(live_blocks * active_two, axis=(0, 1))) / live_count
        scale_two = lax.rsqrt(lax.optimization_barrier(jnp.sum(live_blocks * active_two * active_two, axis=(0, 1))) / live_count - mean_two * mean_two + norm_epsilon)

        def layer_three(inputs):
            block_rows, block_signal, block_live = inputs
            normed = low(norm_rows[2] * ((block_rows - mean_two) * scale_two) + norm_rows[3])
            embedding = low_back(jnp.dot(normed, three_low, precision=highest) + bias_row)
            sent_rows = low(embedding)
            loss_value = jnp.sum(block_signal * sent_rows) + penalty_weight * jnp.sum(block_live * embedding * embedding) / live_count
            return (loss_value, sent_rows)
        losses, sent_rows = lax.map(jax.checkpoint(layer_three), (active_two, signal_blocks, live_blocks))
        return (jnp.sum(losses), sent_rows)
    params = (weight_first, weight_second, weight_final, norm_params, bias_final)
    loss_value, pullback, sent_rows = jax.vjp(total, params, has_aux=True)
    gradients = pullback(jnp.ones_like(loss_value))[0]
    token_embed = sent_rows.reshape(ID_RANGE, OUT_DIM)[token_rows].astype(jnp.bfloat16)
    momentum_first, variance_first, master_first = adam(weight_first, moment_first, square_first, gradients[0], rate_matrix, decay_matrix)
    momentum_second, variance_second, master_second = adam(weight_second, moment_second, square_second, gradients[1], rate_matrix, decay_matrix)
    momentum_final, variance_final, master_final = adam(weight_final, moment_final, square_final, gradients[2], rate_matrix, decay_matrix)
    momentum_norm, variance_norm, master_norm = adam(norm_params, moment_norm, square_norm, gradients[3], rate_norm, 0.0)
    momentum_bias, variance_bias, master_bias = adam(bias_final, moment_bias, square_bias, gradients[4], rate_bias, 0.0)
    return (token_embed, momentum_first, variance_first, master_first, master_first.astype(jnp.bfloat16), momentum_second, variance_second, master_second, master_second.astype(jnp.bfloat16), momentum_final, variance_final, master_final, master_final.astype(jnp.bfloat16), momentum_norm, variance_norm, master_norm, momentum_bias, variance_bias, master_bias)
```

```python
import jax
import jax.numpy as jnp
from jax import lax
from jax.sharding import PartitionSpec as P

STEP = 10


beta_one = 0.9
beta_two = 0.999
adam_epsilon = 1e-08
norm_epsilon = 1e-05
penalty_weight = 0.25
decay_matrix = 0.01
rate_matrix = 0.05
rate_norm = 0.5
rate_bias = 0.02
LANES = 128


def mish_parts(inputs):
    grown = jnp.exp(jnp.minimum(inputs, 20.0))
    above = grown * (grown + 2.0)
    inverse = 1.0 / (above + 2.0)
    return grown, above * inverse, inverse


def mish(inputs):
    return inputs * mish_parts(inputs)[1]


def mish_slope(inputs):
    grown, gate, inverse = mish_parts(inputs)
    return gate + 4.0 * jnp.minimum(inputs, 20.0) * (grown * inverse) * ((1.0 + grown) * inverse)


def contract(left, right, left_dim, right_dim):
    return lax.dot_general(
        left, right, (((left_dim,), (right_dim,)), ((), ())), preferred_element_type=jnp.float32
    )


def norm_back(upstream, unit_rows, gain_row, scale_row, live_mask, gain_sum, shift_sum, live_count):
    return scale_row * (
        gain_row * upstream
        - live_mask[:, None] * gain_row * (shift_sum + unit_rows * gain_sum) / live_count
    )


def adam(weight, moment, square, gradient, step_rate, shrink):
    momentum = beta_one * moment + (1.0 - beta_one) * gradient
    variance = beta_two * square + (1.0 - beta_two) * gradient * gradient
    moment_hat = momentum / (1.0 - beta_one**STEP)
    square_hat = variance / (1.0 - beta_two**STEP)
    master = weight - step_rate * (
        moment_hat / (jnp.sqrt(square_hat) + adam_epsilon) + shrink * weight
    )
    return (momentum, variance, master)


def split_two(values):
    high = values.astype(jnp.bfloat16)
    low = (values - high.astype(jnp.float32)).astype(jnp.bfloat16)
    return high, low


def one_hot(index, length, first):
    rows = lax.broadcasted_iota(jnp.int32, (length, index.shape[0]), 0) + first
    return (rows == index[None, :]).astype(jnp.bfloat16)


def body(
    hash_codes,
    request_ids,
    request_counts,
    token_slots,
    cotangent,
    weight_first,
    weight_second,
    weight_final,
    norm_params,
    bias_final,
    moment_first,
    square_first,
    moment_second,
    square_second,
    moment_final,
    square_final,
    moment_norm,
    square_norm,
    moment_bias,
    square_bias,
):
    owners = lax.axis_size("ids")
    parts = lax.axis_size("mdl")
    part = lax.axis_index("mdl")
    both = ("ids", "mdl")
    range_rows = hash_codes.shape[0]
    rows = range_rows // parts
    slots_per = request_ids.shape[1]
    piece = slots_per // parts
    out_width = weight_final.shape[1]
    width = weight_first.shape[1]
    wide = width + (-width) % LANES
    hidden = wide * parts
    more = wide - width
    token_count = token_slots.shape[0]
    token_piece = token_count // parts
    token_total = token_count * owners

    first_part = jnp.pad(weight_first.astype(jnp.bfloat16), ((0, 0), (0, more)))
    first_low = lax.all_gather(first_part, "ids", axis=0, tiled=True)
    first_low = lax.all_gather(first_low, "mdl", axis=1, tiled=True)
    second_part = jnp.pad(
        weight_second.astype(jnp.bfloat16).reshape(parts, width, width),
        ((0, 0), (0, more), (0, more)),
    ).reshape(hidden, wide)
    second_low = lax.all_gather(second_part, "mdl", axis=1, tiled=True)
    final_part = jnp.pad(weight_final.astype(jnp.bfloat16), ((0, more), (0, 0)))
    final_low = lax.all_gather(final_part, "mdl", axis=0, tiled=True)
    norm_all = lax.all_gather(jnp.pad(norm_params, ((0, 0), (0, more))), "mdl", axis=1, tiled=True)

    encoded = ((hash_codes.astype(jnp.float32) + 0.5) / 512.0 - 1.0).astype(jnp.bfloat16)
    features = lax.all_to_all(encoded, "mdl", split_axis=0, concat_axis=1, tiled=True)

    owner_row = jnp.arange(owners, dtype=jnp.int32)[:, None]
    wanted = jnp.where(
        jnp.arange(slots_per, dtype=jnp.int32)[None, :] < request_counts[:, None],
        request_ids - owner_row * range_rows,
        range_rows,
    )
    received = lax.all_to_all(wanted, "ids", split_axis=0, concat_axis=0, tiled=True)

    slot_owner = token_slots // slots_per
    slot_place = token_slots % slots_per - part * piece
    slot_here = jnp.where(
        (slot_place >= 0) & (slot_place < piece), slot_owner * piece + slot_place, -1
    )
    slot_sum = jnp.dot(
        one_hot(slot_here, owners * piece, 0), cotangent, preferred_element_type=jnp.float32
    ) / token_total
    high, low = split_two(slot_sum)
    sent = jnp.concatenate([high, low], axis=1).reshape(owners, piece * 2 * out_width)
    arrived = lax.all_to_all(sent, "ids", split_axis=0, concat_axis=0, tiled=True)
    arrived = lax.all_gather(arrived.reshape(owners * piece, 2 * out_width), "mdl", axis=0, tiled=False)
    arrived = arrived.reshape(parts * owners * piece, 2 * out_width)
    slot_rows = received.reshape(owners, parts, piece).transpose(1, 0, 2)
    slot_rows = slot_rows.reshape(-1)
    marked = jnp.concatenate(
        [arrived, jnp.ones((arrived.shape[0], 2 * out_width), jnp.bfloat16)], axis=1
    )
    row_sums = jnp.dot(
        one_hot(slot_rows, rows, part * rows), marked, preferred_element_type=jnp.float32
    )
    row_grad = row_sums[:, :out_width] + row_sums[:, out_width : 2 * out_width]
    live_mask = jnp.minimum(row_sums[:, 2 * out_width], 1.0)

    linear_one = jnp.dot(features, first_low, preferred_element_type=jnp.float32)
    active_one = mish(linear_one)
    weighted_one = live_mask[:, None] * active_one
    sums_one = jnp.stack([jnp.sum(weighted_one, 0), jnp.sum(weighted_one * active_one, 0)])
    sums_one, live_count = lax.psum((sums_one, jnp.sum(live_mask)), both)
    mean_one = sums_one[0] / live_count
    scale_one = lax.rsqrt(sums_one[1] / live_count - mean_one * mean_one + norm_epsilon)
    unit_one = (active_one - mean_one) * scale_one
    normed_one = (norm_all[0] * unit_one + norm_all[1]).astype(jnp.bfloat16)
    linear_two = jnp.dot(normed_one, second_low, preferred_element_type=jnp.float32)
    active_two = mish(linear_two)
    weighted_two = live_mask[:, None] * active_two
    sums_two = lax.psum(
        jnp.stack([jnp.sum(weighted_two, 0), jnp.sum(weighted_two * active_two, 0)]), both
    )
    mean_two = sums_two[0] / live_count
    scale_two = lax.rsqrt(sums_two[1] / live_count - mean_two * mean_two + norm_epsilon)
    unit_two = (active_two - mean_two) * scale_two
    normed_two = (norm_all[2] * unit_two + norm_all[3]).astype(jnp.bfloat16)
    embedding = jnp.dot(normed_two, final_low, preferred_element_type=jnp.float32) + bias_final
    embed_low = embedding.astype(jnp.bfloat16)

    embed_range = lax.all_gather(embed_low, "mdl", axis=0, tiled=True)
    slots_mine = lax.dynamic_slice(received, (0, part * piece), (owners, piece)).reshape(-1)
    pick_rows = (
        slots_mine[:, None] == lax.broadcasted_iota(jnp.int32, (owners * piece, range_rows), 1)
    ).astype(jnp.bfloat16)
    replies = jnp.dot(pick_rows, embed_range, preferred_element_type=jnp.float32)
    replies = replies.astype(jnp.bfloat16).reshape(owners, piece * out_width)
    returned = lax.all_to_all(replies, "ids", split_axis=0, concat_axis=0, tiled=True)
    returned = lax.all_gather(returned.reshape(owners, piece, out_width), "mdl", axis=1, tiled=True)
    returned = returned.reshape(owners * slots_per, out_width)
    tokens_mine = lax.dynamic_slice(token_slots, (part * token_piece,), (token_piece,))
    pick_slots = (
        tokens_mine[:, None]
        == lax.broadcasted_iota(jnp.int32, (token_piece, owners * slots_per), 1)
    ).astype(jnp.bfloat16)
    token_part = jnp.dot(pick_slots, returned, preferred_element_type=jnp.float32)
    token_embed = lax.all_gather(token_part.astype(jnp.bfloat16), "mdl", axis=0, tiled=True)

    grad_embed = (
        row_grad + 2.0 * penalty_weight / live_count * live_mask[:, None] * embedding
    ).astype(jnp.bfloat16)
    incoming_two = contract(grad_embed, final_low, 1, 1)
    sums_two = lax.psum(
        jnp.stack([jnp.sum(incoming_two * unit_two, 0), jnp.sum(incoming_two, 0)]), both
    )
    local_final = contract(normed_two, grad_embed, 0, 0)
    local_bias = jnp.sum(grad_embed.astype(jnp.float32), 0)
    outgoing_two = norm_back(
        incoming_two, unit_two, norm_all[2], scale_two, live_mask, sums_two[0], sums_two[1], live_count
    )
    grad_linear_two = (mish_slope(linear_two) * outgoing_two).astype(jnp.bfloat16)
    local_second = jnp.stack(
        [
            contract(normed_one, grad_linear_two[:, wide * k : wide * (k + 1)], 0, 0)
            for k in range(parts)
        ]
    )
    grad_second = lax.psum_scatter(local_second, "mdl", scatter_dimension=0, tiled=False)
    grad_second = lax.psum(grad_second, "ids")
    grad_second = grad_second.reshape(parts, wide, wide)[:, :width, :width].reshape(-1, width)
    incoming_one = contract(grad_linear_two, second_low, 1, 1)
    sums_one, final_sum, grad_bias = lax.psum(
        (
            jnp.stack([jnp.sum(incoming_one * unit_one, 0), jnp.sum(incoming_one, 0)]),
            local_final,
            local_bias,
        ),
        both,
    )
    outgoing_one = norm_back(
        incoming_one, unit_one, norm_all[0], scale_one, live_mask, sums_one[0], sums_one[1], live_count
    )
    grad_linear_one = (mish_slope(linear_one) * outgoing_one).astype(jnp.bfloat16)
    local_first = jnp.stack(
        [
            contract(features, grad_linear_one[:, wide * k : wide * (k + 1)], 0, 0)
            for k in range(parts)
        ]
    )
    grad_first = lax.psum_scatter(local_first, "mdl", scatter_dimension=0, tiled=False)
    grad_first = lax.psum_scatter(grad_first, "ids", scatter_dimension=0, tiled=True)[:, :width]

    start = part * wide
    grad_final = lax.dynamic_slice(final_sum, (start, 0), (width, out_width))
    grad_norm = lax.dynamic_slice(
        jnp.concatenate([sums_one, sums_two]), (0, start), (4, width)
    )
    momentum_first, variance_first, master_first = adam(
        weight_first, moment_first, square_first, grad_first, rate_matrix, decay_matrix
    )
    momentum_second, variance_second, master_second = adam(
        weight_second, moment_second, square_second, grad_second, rate_matrix, decay_matrix
    )
    momentum_final, variance_final, master_final = adam(
        weight_final, moment_final, square_final, grad_final, rate_matrix, decay_matrix
    )
    momentum_norm, variance_norm, master_norm = adam(
        norm_params, moment_norm, square_norm, grad_norm, rate_norm, 0.0
    )
    momentum_bias, variance_bias, master_bias = adam(
        bias_final, moment_bias, square_bias, grad_bias, rate_bias, 0.0
    )
    return (
        token_embed,
        momentum_first,
        variance_first,
        master_first,
        master_first.astype(jnp.bfloat16),
        momentum_second,
        variance_second,
        master_second,
        master_second.astype(jnp.bfloat16),
        momentum_final,
        variance_final,
        master_final,
        master_final.astype(jnp.bfloat16),
        momentum_norm,
        variance_norm,
        master_norm,
        momentum_bias,
        variance_bias,
        master_bias,
    )


def solution(mesh):
    rows = P("ids", None)
    grid = P("ids", "mdl")
    columns = P(None, "mdl")
    mdl_rows = P("mdl", None)
    return jax.shard_map(
        body,
        mesh=mesh,
        in_specs=(grid, rows, P("ids"), P("ids"), rows, grid, columns, mdl_rows, columns, P())
        + (grid,) * 2
        + (columns,) * 2
        + (mdl_rows,) * 2
        + (columns,) * 2
        + (P(),) * 2,
        out_specs=(rows,)
        + (grid,) * 4
        + (columns,) * 4
        + (mdl_rows,) * 4
        + (columns,) * 3
        + (P(),) * 3,
        check_vma=False,
    )
```

```python
import functools
import jax
import jax.numpy as jnp
from jax import lax
from jax.experimental import pallas as pl
from jax.experimental.pallas import tpu as pltpu
from jax.sharding import PartitionSpec as P

STEP = 10


beta_one = 0.9
beta_two = 0.999
adam_epsilon = 1e-08
norm_epsilon = 1e-05
penalty_weight = 0.25
decay_matrix = 0.01
rate_matrix = 0.05
rate_norm = 0.5
rate_bias = 0.02
LANES = 128


def mish_parts(inputs):
    grown = jnp.exp(jnp.minimum(inputs, 20.0))
    above = grown * (grown + 2.0)
    inverse = 1.0 / (above + 2.0)
    return grown, above * inverse, inverse


def mish(inputs):
    return inputs * mish_parts(inputs)[1]


def mish_slope(inputs):
    grown, gate, inverse = mish_parts(inputs)
    return gate + 4.0 * jnp.minimum(inputs, 20.0) * (grown * inverse) * ((1.0 + grown) * inverse)


def contract(left, right, left_dim, right_dim):
    return lax.dot_general(
        left, right, (((left_dim,), (right_dim,)), ((), ())), preferred_element_type=jnp.float32
    )


def norm_back(upstream, unit_rows, gain_row, scale_row, live_mask, gain_sum, shift_sum, live_count):
    return scale_row * (
        gain_row * upstream
        - live_mask[:, None] * gain_row * (shift_sum + unit_rows * gain_sum) / live_count
    )


def adam(weight, moment, square, gradient, step_rate, shrink):
    momentum = beta_one * moment + (1.0 - beta_one) * gradient
    variance = beta_two * square + (1.0 - beta_two) * gradient * gradient
    moment_hat = momentum / (1.0 - beta_one**STEP)
    square_hat = variance / (1.0 - beta_two**STEP)
    master = weight - step_rate * (
        moment_hat / (jnp.sqrt(square_hat) + adam_epsilon) + shrink * weight
    )
    return (momentum, variance, master)


def split_two(values):
    high = values.astype(jnp.bfloat16)
    low = (values - high.astype(jnp.float32)).astype(jnp.bfloat16)
    return high, low


def one_hot(index, length, first):
    rows = lax.broadcasted_iota(jnp.int32, (length, index.shape[0]), 0) + first
    return (rows == index[None, :]).astype(jnp.bfloat16)


MESH = pl.DeviceIdType.MESH
BIG = 60 * 1024 * 1024


def greet(peers):
    barrier = pltpu.get_barrier_semaphore()
    for peer in peers:
        pl.semaphore_signal(barrier, inc=1, device_id=peer, device_id_type=MESH)
    pl.semaphore_wait(barrier, len(peers))


def push(source, target, send_sem, recv_sem, peer):
    return pltpu.make_async_remote_copy(
        src_ref=source,
        dst_ref=target,
        send_sem=send_sem,
        recv_sem=recv_sem,
        device_id=peer,
        device_id_type=MESH,
    )


def gap(axis, size, d):
    return {axis: lax.rem(lax.axis_index(axis) + d, size)}


def exchange_kernel(parts, owners, kinds, *refs):
    extras = len(kinds)
    x_ref, given = refs[0], refs[1 : 1 + extras]
    o_ref, taken = refs[1 + extras], refs[2 + extras : 2 + 2 * extras]
    near, far, send_near, recv_near, send_far, recv_far, *sems = refs[2 + 2 * extras :]
    sizes = {"mdl": parts, "ids": owners}
    part = lax.axis_index("mdl")
    owner = lax.axis_index("ids")
    greet([gap("mdl", parts, d) for d in range(1, parts)] + [gap("ids", owners, d) for d in range(1, owners)])
    copies = [
        push(x_ref, near.at[d], send_near.at[d], recv_near.at[d], gap("mdl", parts, d))
        for d in range(1, parts)
    ]
    for copy in copies:
        copy.start()
    others = []
    for n, (axis, spread) in enumerate(kinds):
        me = lax.axis_index(axis)
        for d in range(1, sizes[axis]):
            peer = gap(axis, sizes[axis], d)
            source = given[n].at[peer[axis]] if spread else given[n]
            copy = push(source, taken[n].at[me], sems[2 * n].at[d], sems[2 * n + 1].at[d], peer)
            copy.start()
            others.append(copy)
        taken[n][me] = given[n][me] if spread else given[n][...]
    near[0] = x_ref[...]
    for copy in copies:
        copy.wait()
    total = near[part]
    for k in range(1, parts):
        total = total + near[lax.rem(part + parts - k, parts)]
    far[0] = total
    copies = [
        push(far.at[0], far.at[d], send_far.at[d], recv_far.at[d], gap("ids", owners, d))
        for d in range(1, owners)
    ]
    for copy in copies:
        copy.start()
    for copy in copies:
        copy.wait()
    total = far[owner]
    for k in range(1, owners):
        total = total + far[lax.rem(owner + owners - k, owners)]
    o_ref[...] = total
    for copy in others:
        copy.wait()


def exchange(x, extras, kinds, call):
    parts, owners = lax.axis_size("mdl"), lax.axis_size("ids")
    sizes = {"mdl": parts, "ids": owners}
    dma = pltpu.SemaphoreType.DMA
    whole = pl.BlockSpec(memory_space=pltpu.VMEM)
    outs = [jax.ShapeDtypeStruct(x.shape, jnp.float32)]
    sems = []
    for extra, (axis, spread) in zip(extras, kinds):
        shape = extra.shape if spread else (sizes[axis],) + extra.shape
        outs.append(jax.ShapeDtypeStruct(shape, extra.dtype))
        sems += [dma((sizes[axis],)), dma((sizes[axis],))]
    return pl.pallas_call(
        functools.partial(exchange_kernel, parts, owners, kinds),
        out_shape=tuple(outs),
        in_specs=[whole] * (1 + len(extras)),
        out_specs=(whole,) * len(outs),
        scratch_shapes=[
            pltpu.VMEM((parts,) + x.shape, jnp.float32),
            pltpu.VMEM((owners,) + x.shape, jnp.float32),
            dma((parts,)),
            dma((parts,)),
            dma((owners,)),
            dma((owners,)),
        ]
        + sems,
        compiler_params=pltpu.CompilerParams(collective_id=call, has_side_effects=True),
        name="exchange",
    )(x, *extras)


def front_kernel(
    parts, owners, first, codes, norms, final, wanted, weights, feats, norms_all, final_all, received,
    s1, r1, s2, r2, s3, r3, sc, rc, sn, rn, sw, rw, sl,
):
    part = lax.axis_index("mdl")
    owner = lax.axis_index("ids")
    pair = {"mdl": part + 1 - 2 * lax.rem(part, 2)}
    cross_part = lax.rem(part + 2, parts)
    cross = {"mdl": cross_part}
    rows, width = first.shape
    codes_width = codes.shape[2]
    greet([gap("mdl", parts, d) for d in range(1, parts)] + [gap("ids", owners, d) for d in range(1, owners)])

    def spot(who, which):
        return weights.at[
            pl.ds(pl.multiple_of(who * rows, rows), rows),
            pl.ds(pl.multiple_of(which * width, width), width),
        ]

    mine = feats.at[:, pl.ds(pl.multiple_of(part * codes_width, codes_width), codes_width)]
    locals_ = [
        pltpu.make_async_copy(first, spot(owner, part), sl.at[0]),
        pltpu.make_async_copy(codes.at[part], mine, sl.at[1]),
    ]
    for copy in locals_:
        copy.start()
    ones, lines = [], []
    for d in range(1, owners):
        peer = gap("ids", owners, d)
        copy = push(first, spot(owner, part), s1.at[d], r1.at[d], peer)
        copy.start()
        ones.append(copy)
        copy = push(wanted.at[peer["ids"]], received.at[owner], sw.at[d], rw.at[d], peer)
        copy.start()
        lines.append(copy)
    for d in range(1, parts):
        peer = gap("mdl", parts, d)
        for n, (source, target) in enumerate(((norms, norms_all), (final, final_all))):
            copy = push(source, target.at[part], sn.at[n, d], rn.at[n, d], peer)
            copy.start()
            lines.append(copy)
    for d in range(1, parts):
        peer = gap("mdl", parts, d)
        copy = push(codes.at[peer["mdl"]], mine, sc.at[d], rc.at[d], peer)
        copy.start()
        lines.append(copy)
    received[owner] = wanted[owner]
    norms_all[part] = norms[...]
    final_all[part] = final[...]
    twos, threes = [], []
    for d in range(owners):
        who = lax.rem(owner + owners - d, owners)
        if d == 0:
            locals_[0].wait()
        else:
            ones[d - 1].wait_send()
            push(first, spot(who, part), s1.at[d], r1.at[d], pair).wait_recv()
        piece = spot(who, part)
        copy = push(piece, piece, s2.at[d], r2.at[d], cross)
        copy.start()
        twos.append(copy)
        copy = push(piece, piece, s3.at[0, d], r3.at[0, d], pair)
        copy.start()
        threes.append(copy)
    for d in range(owners):
        who = lax.rem(owner + owners - d, owners)
        twos[d].wait_send()
        piece = spot(who, cross_part)
        push(piece, piece, s2.at[d], r2.at[d], cross).wait_recv()
        copy = push(piece, piece, s3.at[1, d], r3.at[1, d], pair)
        copy.start()
        threes.append(copy)
    for copy in threes + lines:
        copy.wait()
    locals_[1].wait()


def front(first, codes, norms, final, wanted, call):
    parts, owners = lax.axis_size("mdl"), lax.axis_size("ids")
    dma = pltpu.SemaphoreType.DMA
    held = pl.BlockSpec(memory_space=pl.ANY)
    whole = pl.BlockSpec(memory_space=pltpu.VMEM)
    shape = jax.ShapeDtypeStruct
    return pl.pallas_call(
        functools.partial(front_kernel, parts, owners),
        out_shape=(
            shape((first.shape[0] * owners, first.shape[1] * parts), first.dtype),
            shape((codes.shape[1], codes.shape[2] * parts), codes.dtype),
            shape((parts,) + norms.shape, norms.dtype),
            shape((parts,) + final.shape, final.dtype),
            shape(wanted.shape, wanted.dtype),
        ),
        in_specs=[whole] * 5,
        out_specs=(held, held, whole, whole, whole),
        scratch_shapes=[dma((owners,))] * 4
        + [dma((2, owners))] * 2
        + [dma((parts,))] * 2
        + [dma((2, parts))] * 2
        + [dma((owners,))] * 2
        + [dma((2,))],
        compiler_params=pltpu.CompilerParams(collective_id=call, has_side_effects=True, vmem_limit_bytes=16 * 1024 * 1024),
        name="front",
    )(first, codes, norms, final, wanted)


def blocks(count, step, body):
    if count == step:
        body(0)
    else:
        @pl.loop(0, count // step)
        def _(k):
            body(pl.multiple_of(k * step, step))


NAMES = (
    "own",
    "got",
    "out_y",
    "in_y",
    "out_f",
    "in_f",
    "s0",
    "r0",
    "sl",
    "sy",
    "ry",
    "sf",
    "rf",
    "sg",
    "rg",
    "st",
    "rt",
)


class Unit:
    pass


def reduce_kernel(parts, owners, plan, *refs):
    half = parts // 2
    count = len(plan)
    inputs, (replies, picks) = refs[:count], refs[count : count + 2]
    outputs, tokens_out = refs[count + 2 : 2 * count + 2], refs[2 * count + 2]
    scratch = list(refs[2 * count + 3 :])
    gathered, made, sp, rp, st_, rt_ = scratch[:6]
    scratch = scratch[6:]
    part = lax.axis_index("mdl")
    owner = lax.axis_index("ids")
    low, place = lax.rem(part, 2), part // 2
    pair = {"mdl": part + 1 - 2 * low}
    cross = {"mdl": lax.rem(part + 2, parts)}
    side, row = lax.rem(owner, 2), owner // 2
    twin = {"ids": owner + 1 - 2 * side}
    line = owners // 2
    units = []
    for n, (rows, lanes, chunks, keep, wire) in enumerate(plan):
        bufs = {name: scratch.pop(0) for name in NAMES[: 17 if keep else 13]}
        for c in range(chunks):
            u = Unit()
            u.__dict__.update(bufs)
            u.rows, u.lanes, u.width, u.keep, u.c, u.wire = rows, lanes, lanes // chunks, keep, c, wire
            u.piece = rows // owners
            u.cols = pl.ds(c * u.width, u.width)
            u.source, u.out = inputs[n], outputs[n]
            units.append(u)
    greet([gap("mdl", parts, d) for d in range(1, parts)] + [gap("ids", owners, d) for d in range(1, owners)])

    def taken(u, k):
        if len(u.source.shape) == 3:
            return u.source.at[k, :, u.cols]
        start = pl.multiple_of(k * u.lanes + u.c * u.width, u.width)
        return u.source.at[:, pl.ds(start, u.width)]

    def begin(u):
        u.first, u.mine = [], []
        for i in range(half):
            u.first.append(
                push(
                    taken(u, 1 - low + 2 * i),
                    u.got.at[i, :, u.cols],
                    u.s0.at[u.c, i],
                    u.r0.at[u.c, i],
                    pair,
                )
            )
            u.mine.append(
                pltpu.make_async_copy(
                    taken(u, low + 2 * i), u.own.at[i, :, u.cols], u.sl.at[u.c, i]
                )
            )
        for copy in u.first + u.mine:
            copy.start()

    def sweep(u, body):
        step = min(u.rows, 64)
        blocks(u.rows, step, lambda k: body((pl.ds(k, step), u.cols)))

    def to_cross(u):
        for copy in u.first + u.mine:
            copy.wait()

        def body(at):
            spot = (1 - place,) + at
            u.out_y[at] = (u.own[spot] + u.got[spot]).astype(u.wire)

        sweep(u, body)
        u.second = push(
            u.out_y.at[:, u.cols], u.in_y.at[:, u.cols], u.sy.at[u.c], u.ry.at[u.c], cross
        )
        u.second.start()

    def to_owners(u):
        u.second.wait()

        def body(at):
            spot = (place,) + at
            value = u.own[spot] + u.got[spot] + u.in_y[at].astype(jnp.float32)
            u.own[spot] = value
            u.out_f[at] = value.astype(u.wire)

        sweep(u, body)
        u.third = []
        for d in range(1, owners):
            peer = lax.rem(owner + d, owners)
            copy = push(
                u.out_f.at[pl.ds(pl.multiple_of(peer * u.piece, u.piece), u.piece), u.cols],
                u.in_f.at[d, :, u.cols],
                u.sf.at[u.c, d],
                u.rf.at[u.c, d],
                {"ids": peer},
            )
            copy.start()
            u.third.append(copy)

    def finish(u):
        for copy in u.third:
            copy.wait()
        here = pl.ds(pl.multiple_of(owner * u.piece, u.piece), u.piece)
        value = u.own[place, here, u.cols]
        for d in range(1, owners):
            value = value + u.in_f[d, :, u.cols].astype(jnp.float32)
        if not u.keep:
            u.out[:, u.cols] = value
            return
        u.out[row, side, :, u.cols] = value
        u.fourth = []
        spot = u.out.at[row, side, :, u.cols]
        for d in range(1, line):
            peer = {"ids": lax.rem(row + d, line) * 2 + side}
            copy = push(spot, spot, u.sg.at[u.c, d], u.rg.at[u.c, d], peer)
            copy.start()
            u.fourth.append(copy)

    def to_twin(u):
        if not u.keep:
            return
        for d, copy in zip(range(1, line), u.fourth):
            copy.wait_send()
            there = u.out.at[lax.rem(row + line - d, line), side, :, u.cols]
            push(there, there, u.sg.at[u.c, d], u.rg.at[u.c, d], twin).wait_recv()
        spot = u.out.at[:, side, :, u.cols]
        u.fifth = push(spot, spot, u.st.at[u.c], u.rt.at[u.c], twin)
        u.fifth.start()

    def close(u):
        if not u.keep:
            return
        u.fifth.wait_send()
        there = u.out.at[:, 1 - side, :, u.cols]
        push(there, there, u.st.at[u.c], u.rt.at[u.c], twin).wait_recv()

    def share(source, target, send, recv):
        copies = [
            push(source, target.at[part], send.at[d], recv.at[d], gap("mdl", parts, d))
            for d in range(1, parts)
        ]
        for copy in copies:
            copy.start()
        return copies

    piece = replies.shape[2]
    slots = piece * parts

    def select(q):
        def body(j, summed):
            first = j * slots + q * piece
            place_ = lax.broadcasted_iota(jnp.int32, (piece, picks.shape[1]), 0) + first
            chosen = jnp.where(place_ == picks[...], 1.0, 0.0).astype(jnp.bfloat16)
            return summed + jnp.dot(gathered[q, j], chosen, preferred_element_type=jnp.float32)

        start = jnp.zeros((replies.shape[1], picks.shape[1]), jnp.float32)
        summed = lax.fori_loop(0, owners, body, start)
        made[...] = summed.astype(jnp.bfloat16) if q == 0 else made[...] + summed.astype(jnp.bfloat16)

    early = share(replies, gathered, sp, rp)
    gathered[part] = replies[...]
    for u in units:
        begin(u)
    total = len(units)
    late = []
    stages = (to_cross, to_owners, finish, to_twin, close)
    for t in range(total + len(stages) - 1):
        for s, stage in enumerate(stages):
            if 0 <= t - s < total:
                stage(units[t - s])
        if t == 0:
            for copy in early:
                copy.wait()
        if t < parts:
            select(t)
        if t == parts - 1:
            tokens_out[part] = made[...]
            late = share(made, tokens_out, st_, rt_)
    for copy in late:
        copy.wait()


def reduce_grads(arrays, plan, replies, picks, call):
    parts, owners = lax.axis_size("mdl"), lax.axis_size("ids")
    half = parts // 2
    found_shape = (replies.shape[1], picks.shape[1])
    outs = []
    scratch = [
        pltpu.VMEM((parts,) + replies.shape, replies.dtype),
        pltpu.VMEM(found_shape, replies.dtype),
    ] + [pltpu.SemaphoreType.DMA((parts,))] * 4
    for rows, lanes, chunks, keep, wire in plan:
        piece = rows // owners
        outs.append(
            jax.ShapeDtypeStruct(
                (owners // 2, 2, piece, lanes) if keep else (piece, lanes), jnp.float32
            )
        )
        dma = pltpu.SemaphoreType.DMA
        scratch += [
            pltpu.VMEM((half, rows, lanes), jnp.float32),
            pltpu.VMEM((half, rows, lanes), jnp.float32),
            pltpu.VMEM((rows, lanes), wire),
            pltpu.VMEM((rows, lanes), wire),
            pltpu.VMEM((rows, lanes), wire),
            pltpu.VMEM((owners, piece, lanes), wire),
            dma((chunks, half)),
            dma((chunks, half)),
            dma((chunks, half)),
            dma((chunks,)),
            dma((chunks,)),
            dma((chunks, owners)),
            dma((chunks, owners)),
        ]
        if keep:
            scratch += [
                dma((chunks, owners // 2)),
                dma((chunks, owners // 2)),
                dma((chunks,)),
                dma((chunks,)),
            ]
    found = pl.pallas_call(
        functools.partial(reduce_kernel, parts, owners, plan),
        out_shape=tuple(outs) + (jax.ShapeDtypeStruct((parts,) + found_shape, replies.dtype),),
        in_specs=[pl.BlockSpec(memory_space=pl.ANY)] * len(arrays)
        + [pl.BlockSpec(memory_space=pltpu.VMEM)] * 2,
        out_specs=(pl.BlockSpec(memory_space=pltpu.VMEM),) * (len(arrays) + 1),
        scratch_shapes=scratch,
        compiler_params=pltpu.CompilerParams(
            collective_id=call, has_side_effects=True, vmem_limit_bytes=BIG
        ),
        name="reduce_grads",
    )(*arrays, replies, picks)
    return tuple(v.reshape(-1, v.shape[-1]) for v in found[:-1]) + (found[-1],)


def total(vectors, small, extras, kinds, call):
    rows = [v.reshape(-1, LANES) for v in vectors]
    sizes = [r.shape[0] for r in rows]
    if small is not None:
        rows.append(jnp.pad(small.reshape(1, -1), ((0, 7), (0, LANES - small.size))))
    summed, *moved = exchange(jnp.concatenate(rows, axis=0), extras, kinds, call)
    found, start = [], 0
    for size in sizes:
        found.append(summed[start : start + size].reshape(-1))
        start += size
    if small is not None:
        found.append(summed[start, : small.size])
    return found, moved


def body(
    hash_codes,
    request_ids,
    request_counts,
    token_slots,
    cotangent,
    weight_first,
    weight_second,
    weight_final,
    norm_params,
    bias_final,
    moment_first,
    square_first,
    moment_second,
    square_second,
    moment_final,
    square_final,
    moment_norm,
    square_norm,
    moment_bias,
    square_bias,
):
    owners = lax.axis_size("ids")
    parts = lax.axis_size("mdl")
    part = lax.axis_index("mdl")
    range_rows = hash_codes.shape[0]
    rows = range_rows // parts
    slots_per = request_ids.shape[1]
    piece = slots_per // parts
    out_width = weight_final.shape[1]
    width = weight_first.shape[1]
    wide = width + (-width) % LANES
    hidden = wide * parts
    more = wide - width
    token_count = token_slots.shape[0]
    token_piece = token_count // parts
    token_total = token_count * owners

    encoded = ((hash_codes.astype(jnp.float32) + 0.5) / 512.0 - 1.0).astype(jnp.bfloat16)
    owner_row = jnp.arange(owners, dtype=jnp.int32)[:, None]
    wanted = jnp.where(
        jnp.arange(slots_per, dtype=jnp.int32)[None, :] < request_counts[:, None],
        request_ids - owner_row * range_rows,
        range_rows,
    )
    first_low, features, norm_all, final_all, received = front(
        jnp.pad(weight_first.astype(jnp.bfloat16), ((0, 0), (0, more))),
        encoded.reshape(parts, rows, -1),
        jnp.pad(norm_params, ((0, 4), (0, more))),
        jnp.pad(weight_final.astype(jnp.bfloat16).T, ((0, 0), (0, more))),
        wanted.reshape(owners, 1, slots_per),
        5,
    )
    norm_all = norm_all.transpose(1, 0, 2).reshape(-1, hidden)[:4]
    final_low = final_all.transpose(1, 0, 2).reshape(out_width, hidden)
    second_part = jnp.pad(
        weight_second.astype(jnp.bfloat16).reshape(parts, width, width),
        ((0, 0), (0, more), (0, more)),
    ).reshape(hidden, wide)
    second_part, first_low = lax.optimization_barrier((second_part, first_low))
    second_low = lax.all_gather(second_part, "mdl", axis=1, tiled=True)

    received = received.reshape(owners, slots_per)
    here = part * rows + jnp.arange(rows, dtype=jnp.int32)
    live_mask = jnp.max(
        (received.reshape(1, -1) == here[:, None]).astype(jnp.float32), axis=1
    )
    slots_mine = lax.dynamic_slice(received, (0, part * piece), (owners, piece)).reshape(-1)
    pick_rows = (
        slots_mine[:, None] == lax.broadcasted_iota(jnp.int32, (owners * piece, range_rows), 1)
    ).astype(jnp.bfloat16)

    slot_owner = token_slots // slots_per
    slot_place = token_slots % slots_per - part * piece
    slot_here = jnp.where(
        (slot_place >= 0) & (slot_place < piece), slot_owner * piece + slot_place, -1
    )
    slot_sum = contract(cotangent, one_hot(slot_here, owners * piece, 0), 0, 1) / token_total
    sent = jnp.concatenate(split_two(slot_sum), axis=0)
    sent = sent.reshape(2 * out_width, owners, piece).transpose(1, 0, 2)

    linear_one = jnp.dot(features, first_low, preferred_element_type=jnp.float32)
    active_one = mish(linear_one)
    weighted_one = live_mask[:, None] * active_one
    (*sums_one, live_count), (arrived,) = total(
        [jnp.sum(weighted_one, 0), jnp.sum(weighted_one * active_one, 0)],
        jnp.sum(live_mask).reshape(1),
        [sent],
        (("ids", True),),
        0,
    )
    live_count = live_count[0]
    mean_one = sums_one[0] / live_count
    scale_one = lax.rsqrt(sums_one[1] / live_count - mean_one * mean_one + norm_epsilon)
    unit_one = (active_one - mean_one) * scale_one
    normed_one = (norm_all[0] * unit_one + norm_all[1]).astype(jnp.bfloat16)
    arrived = arrived.transpose(1, 0, 2).reshape(2 * out_width, owners * piece)
    row_part = jnp.dot(arrived, pick_rows, preferred_element_type=jnp.float32)
    row_part = (row_part[:out_width] + row_part[out_width:]).reshape(out_width, parts, rows)
    linear_two = jnp.dot(normed_one, second_low, preferred_element_type=jnp.float32)
    active_two = mish(linear_two)
    weighted_two = live_mask[:, None] * active_two
    sums_two, (row_parts,) = total(
        [jnp.sum(weighted_two, 0), jnp.sum(weighted_two * active_two, 0)],
        None,
        [row_part.transpose(1, 0, 2)],
        (("mdl", True),),
        1,
    )
    row_grad = jnp.sum(row_parts, 0)
    mean_two = sums_two[0] / live_count
    scale_two = lax.rsqrt(sums_two[1] / live_count - mean_two * mean_two + norm_epsilon)
    unit_two = (active_two - mean_two) * scale_two
    normed_two = (norm_all[2] * unit_two + norm_all[3]).astype(jnp.bfloat16)
    embedding = contract(final_low, normed_two, 1, 1) + bias_final[:, None]

    grad_embed = (
        row_grad + 2.0 * penalty_weight / live_count * live_mask[None, :] * embedding
    ).astype(jnp.bfloat16)
    incoming_two = contract(grad_embed, final_low, 0, 0)
    (*sums_two, grad_bias), (embed_range,) = total(
        [jnp.sum(incoming_two * unit_two, 0), jnp.sum(incoming_two, 0)],
        jnp.sum(grad_embed.astype(jnp.float32), 1),
        [embedding.astype(jnp.bfloat16)],
        (("mdl", False),),
        2,
    )
    embed_range = embed_range.transpose(1, 0, 2).reshape(out_width, range_rows)
    replies = contract(embed_range, pick_rows, 1, 1).astype(jnp.bfloat16)
    replies = replies.reshape(out_width, owners, piece).transpose(1, 0, 2)
    local_final = jnp.pad(
        contract(normed_two, grad_embed, 0, 1).reshape(parts, wide, out_width),
        ((0, 0), (0, 0), (0, (-out_width) % LANES)),
    )
    outgoing_two = norm_back(
        incoming_two, unit_two, norm_all[2], scale_two, live_mask, sums_two[0], sums_two[1], live_count
    )
    grad_linear_two = (mish_slope(linear_two) * outgoing_two).astype(jnp.bfloat16)
    local_second = contract(grad_linear_two, normed_one, 0, 0).reshape(parts, wide, hidden)
    incoming_one = contract(grad_linear_two, second_low, 1, 1)
    sums_one, (returned,) = total(
        [jnp.sum(incoming_one * unit_one, 0), jnp.sum(incoming_one, 0)],
        None,
        [replies],
        (("ids", True),),
        3,
    )
    outgoing_one = norm_back(
        incoming_one, unit_one, norm_all[0], scale_one, live_mask, sums_one[0], sums_one[1], live_count
    )
    grad_linear_one = (mish_slope(linear_one) * outgoing_one).astype(jnp.bfloat16)
    local_first = contract(features, grad_linear_one, 0, 0)
    tokens_mine = lax.dynamic_slice(token_slots, (part * token_piece,), (token_piece,))
    second_sum, final_sum, first_sum, tokens = reduce_grads(
        (local_second, local_final, local_first),
        (
            (wide, hidden, 8, True, jnp.bfloat16),
            (wide, local_final.shape[2], 1, True, jnp.float32),
            (features.shape[1], wide, 2, False, jnp.bfloat16),
        ),
        returned,
        tokens_mine.reshape(1, token_piece),
        4,
    )
    token_embed = tokens.transpose(0, 2, 1).reshape(token_count, out_width)
    grad_second = second_sum[:width].reshape(width, parts, wide)
    grad_second = grad_second[:, :, :width].reshape(width, parts * width).T
    grad_final = final_sum[:width, :out_width]
    grad_first = first_sum[:, :width]
    start = part * wide
    grad_norm = lax.dynamic_slice(jnp.stack([*sums_one, *sums_two]), (0, start), (4, width))
    momentum_first, variance_first, master_first = adam(
        weight_first, moment_first, square_first, grad_first, rate_matrix, decay_matrix
    )
    momentum_second, variance_second, master_second = adam(
        weight_second, moment_second, square_second, grad_second, rate_matrix, decay_matrix
    )
    momentum_final, variance_final, master_final = adam(
        weight_final, moment_final, square_final, grad_final, rate_matrix, decay_matrix
    )
    momentum_norm, variance_norm, master_norm = adam(
        norm_params, moment_norm, square_norm, grad_norm, rate_norm, 0.0
    )
    momentum_bias, variance_bias, master_bias = adam(
        bias_final, moment_bias, square_bias, grad_bias, rate_bias, 0.0
    )
    return (
        token_embed,
        momentum_first,
        variance_first,
        master_first,
        master_first.astype(jnp.bfloat16),
        momentum_second,
        variance_second,
        master_second,
        master_second.astype(jnp.bfloat16),
        momentum_final,
        variance_final,
        master_final,
        master_final.astype(jnp.bfloat16),
        momentum_norm,
        variance_norm,
        master_norm,
        momentum_bias,
        variance_bias,
        master_bias,
    )


def solution(mesh):
    rows = P("ids", None)
    grid = P("ids", "mdl")
    columns = P(None, "mdl")
    mdl_rows = P("mdl", None)
    return jax.shard_map(
        body,
        mesh=mesh,
        in_specs=(grid, rows, P("ids"), P("ids"), rows, grid, columns, mdl_rows, columns, P())
        + (grid,) * 2
        + (columns,) * 2
        + (mdl_rows,) * 2
        + (columns,) * 2
        + (P(),) * 2,
        out_specs=(rows,)
        + (grid,) * 4
        + (columns,) * 4
        + (mdl_rows,) * 4
        + (columns,) * 3
        + (P(),) * 3,
        check_vma=False,
    )
```

```python
import functools
import jax
import jax.numpy as jnp
from jax import lax
from jax.experimental import pallas as pl
from jax.experimental.pallas import tpu as pltpu
from jax.sharding import PartitionSpec as P

STEP = 10


beta_one = 0.9
beta_two = 0.999
adam_epsilon = 1e-08
norm_epsilon = 1e-05
penalty_weight = 0.25
decay_matrix = 0.01
rate_matrix = 0.05
rate_norm = 0.5
rate_bias = 0.02
LANES = 128


def mish_parts(inputs):
    grown = jnp.exp(jnp.minimum(inputs, 20.0))
    above = grown * (grown + 2.0)
    inverse = 1.0 / (above + 2.0)
    return grown, above * inverse, inverse


def mish(inputs):
    return inputs * mish_parts(inputs)[1]


def mish_slope(inputs):
    grown, gate, inverse = mish_parts(inputs)
    return gate + 4.0 * jnp.minimum(inputs, 20.0) * (grown * inverse) * ((1.0 + grown) * inverse)


def contract(left, right, left_dim, right_dim):
    return lax.dot_general(
        left, right, (((left_dim,), (right_dim,)), ((), ())), preferred_element_type=jnp.float32
    )


def norm_back(upstream, unit_rows, gain_row, scale_row, live_mask, gain_sum, shift_sum, live_count):
    return scale_row * (
        gain_row * upstream
        - live_mask[:, None] * gain_row * (shift_sum + unit_rows * gain_sum) / live_count
    )


def adam(weight, moment, square, gradient, step_rate, shrink):
    momentum = beta_one * moment + (1.0 - beta_one) * gradient
    variance = beta_two * square + (1.0 - beta_two) * gradient * gradient
    moment_hat = momentum / (1.0 - beta_one**STEP)
    square_hat = variance / (1.0 - beta_two**STEP)
    master = weight - step_rate * (
        moment_hat / (jnp.sqrt(square_hat) + adam_epsilon) + shrink * weight
    )
    return (momentum, variance, master)


def split_two(values):
    high = values.astype(jnp.bfloat16)
    low = (values - high.astype(jnp.float32)).astype(jnp.bfloat16)
    return high, low


def one_hot(index, length, first):
    rows = lax.broadcasted_iota(jnp.int32, (length, index.shape[0]), 0) + first
    return (rows == index[None, :]).astype(jnp.bfloat16)


MESH = pl.DeviceIdType.MESH


def greet(peers):
    barrier = pltpu.get_barrier_semaphore()
    for peer in peers:
        pl.semaphore_signal(barrier, inc=1, device_id=peer, device_id_type=MESH)
    pl.semaphore_wait(barrier, len(peers))


def push(source, target, send_sem, recv_sem, peer):
    return pltpu.make_async_remote_copy(
        src_ref=source,
        dst_ref=target,
        send_sem=send_sem,
        recv_sem=recv_sem,
        device_id=peer,
        device_id_type=MESH,
    )


def gap(axis, size, d):
    return {axis: lax.rem(lax.axis_index(axis) + d, size)}


def exchange_kernel(parts, owners, kinds, *refs):
    extras = len(kinds)
    x_ref, given = refs[0], refs[1 : 1 + extras]
    o_ref, taken = refs[1 + extras], refs[2 + extras : 2 + 2 * extras]
    near, far, send_near, recv_near, send_far, recv_far, *sems = refs[2 + 2 * extras :]
    sizes = {"mdl": parts, "ids": owners}
    part = lax.axis_index("mdl")
    owner = lax.axis_index("ids")
    greet([gap("mdl", parts, d) for d in range(1, parts)] + [gap("ids", owners, d) for d in range(1, owners)])
    copies = [
        push(x_ref, near.at[d], send_near.at[d], recv_near.at[d], gap("mdl", parts, d))
        for d in range(1, parts)
    ]
    for copy in copies:
        copy.start()
    others = []
    for n, (axis, spread) in enumerate(kinds):
        me = lax.axis_index(axis)
        for d in range(1, sizes[axis]):
            peer = gap(axis, sizes[axis], d)
            source = given[n].at[peer[axis]] if spread else given[n]
            copy = push(source, taken[n].at[me], sems[2 * n].at[d], sems[2 * n + 1].at[d], peer)
            copy.start()
            others.append(copy)
        taken[n][me] = given[n][me] if spread else given[n][...]
    near[0] = x_ref[...]
    for copy in copies:
        copy.wait()
    total = near[part]
    for k in range(1, parts):
        total = total + near[lax.rem(part + parts - k, parts)]
    far[0] = total
    copies = [
        push(far.at[0], far.at[d], send_far.at[d], recv_far.at[d], gap("ids", owners, d))
        for d in range(1, owners)
    ]
    for copy in copies:
        copy.start()
    for copy in copies:
        copy.wait()
    total = far[owner]
    for k in range(1, owners):
        total = total + far[lax.rem(owner + owners - k, owners)]
    o_ref[...] = total
    for copy in others:
        copy.wait()


def exchange(x, extras, kinds, call):
    parts, owners = lax.axis_size("mdl"), lax.axis_size("ids")
    sizes = {"mdl": parts, "ids": owners}
    dma = pltpu.SemaphoreType.DMA
    whole = pl.BlockSpec(memory_space=pltpu.VMEM)
    outs = [jax.ShapeDtypeStruct(x.shape, jnp.float32)]
    sems = []
    for extra, (axis, spread) in zip(extras, kinds):
        shape = extra.shape if spread else (sizes[axis],) + extra.shape
        outs.append(jax.ShapeDtypeStruct(shape, extra.dtype))
        sems += [dma((sizes[axis],)), dma((sizes[axis],))]
    return pl.pallas_call(
        functools.partial(exchange_kernel, parts, owners, kinds),
        out_shape=tuple(outs),
        in_specs=[whole] * (1 + len(extras)),
        out_specs=(whole,) * len(outs),
        scratch_shapes=[
            pltpu.VMEM((parts,) + x.shape, jnp.float32),
            pltpu.VMEM((owners,) + x.shape, jnp.float32),
            dma((parts,)),
            dma((parts,)),
            dma((owners,)),
            dma((owners,)),
        ]
        + sems,
        compiler_params=pltpu.CompilerParams(collective_id=call, has_side_effects=True),
        name="exchange",
    )(x, *extras)


def front_kernel(
    parts, owners, first, codes, norms, final, wanted, weights, feats, norms_all, final_all, received,
    s1, r1, s2, r2, s3, r3, sc, rc, sn, rn, sw, rw, sl,
):
    part = lax.axis_index("mdl")
    owner = lax.axis_index("ids")
    pair = {"mdl": part + 1 - 2 * lax.rem(part, 2)}
    cross_part = lax.rem(part + 2, parts)
    cross = {"mdl": cross_part}
    rows, width = first.shape
    codes_width = codes.shape[2]
    greet([gap("mdl", parts, d) for d in range(1, parts)] + [gap("ids", owners, d) for d in range(1, owners)])

    def spot(who, which):
        return weights.at[
            pl.ds(pl.multiple_of(who * rows, rows), rows),
            pl.ds(pl.multiple_of(which * width, width), width),
        ]

    mine = feats.at[:, pl.ds(pl.multiple_of(part * codes_width, codes_width), codes_width)]
    locals_ = [
        pltpu.make_async_copy(first, spot(owner, part), sl.at[0]),
        pltpu.make_async_copy(codes.at[part], mine, sl.at[1]),
    ]
    for copy in locals_:
        copy.start()
    ones, lines = [], []
    for d in range(1, owners):
        peer = gap("ids", owners, d)
        copy = push(first, spot(owner, part), s1.at[d], r1.at[d], peer)
        copy.start()
        ones.append(copy)
        copy = push(wanted.at[peer["ids"]], received.at[owner], sw.at[d], rw.at[d], peer)
        copy.start()
        lines.append(copy)
    for d in range(1, parts):
        peer = gap("mdl", parts, d)
        for n, (source, target) in enumerate(((norms, norms_all), (final, final_all))):
            copy = push(source, target.at[part], sn.at[n, d], rn.at[n, d], peer)
            copy.start()
            lines.append(copy)
    for d in range(1, parts):
        peer = gap("mdl", parts, d)
        copy = push(codes.at[peer["mdl"]], mine, sc.at[d], rc.at[d], peer)
        copy.start()
        lines.append(copy)
    received[owner] = wanted[owner]
    norms_all[part] = norms[...]
    final_all[part] = final[...]
    twos, threes = [], []
    for d in range(owners):
        who = lax.rem(owner + owners - d, owners)
        if d == 0:
            locals_[0].wait()
        else:
            ones[d - 1].wait_send()
            push(first, spot(who, part), s1.at[d], r1.at[d], pair).wait_recv()
        piece = spot(who, part)
        copy = push(piece, piece, s2.at[d], r2.at[d], cross)
        copy.start()
        twos.append(copy)
        copy = push(piece, piece, s3.at[0, d], r3.at[0, d], pair)
        copy.start()
        threes.append(copy)
    for d in range(owners):
        who = lax.rem(owner + owners - d, owners)
        twos[d].wait_send()
        piece = spot(who, cross_part)
        push(piece, piece, s2.at[d], r2.at[d], cross).wait_recv()
        copy = push(piece, piece, s3.at[1, d], r3.at[1, d], pair)
        copy.start()
        threes.append(copy)
    for copy in threes + lines:
        copy.wait()
    locals_[1].wait()


def front(first, codes, norms, final, wanted, call):
    parts, owners = lax.axis_size("mdl"), lax.axis_size("ids")
    dma = pltpu.SemaphoreType.DMA
    held = pl.BlockSpec(memory_space=pl.ANY)
    whole = pl.BlockSpec(memory_space=pltpu.VMEM)
    shape = jax.ShapeDtypeStruct
    return pl.pallas_call(
        functools.partial(front_kernel, parts, owners),
        out_shape=(
            shape((first.shape[0] * owners, first.shape[1] * parts), first.dtype),
            shape((codes.shape[1], codes.shape[2] * parts), codes.dtype),
            shape((parts,) + norms.shape, norms.dtype),
            shape((parts,) + final.shape, final.dtype),
            shape(wanted.shape, wanted.dtype),
        ),
        in_specs=[whole] * 5,
        out_specs=(held, held, whole, whole, whole),
        scratch_shapes=[dma((owners,))] * 4
        + [dma((2, owners))] * 2
        + [dma((parts,))] * 2
        + [dma((2, parts))] * 2
        + [dma((owners,))] * 2
        + [dma((2,))],
        compiler_params=pltpu.CompilerParams(collective_id=call, has_side_effects=True, vmem_limit_bytes=16 * 1024 * 1024),
        name="front",
    )(first, codes, norms, final, wanted)


def blocks(count, step, body):
    if count == step:
        body(0)
    else:
        @pl.loop(0, count // step)
        def _(k):
            body(pl.multiple_of(k * step, step))


NAMES = (
    "own",
    "got",
    "out_y",
    "in_y",
    "out_f",
    "in_f",
    "s0",
    "r0",
    "sl",
    "sy",
    "ry",
    "sf",
    "rf",
    "sg",
    "rg",
    "st",
    "rt",
)


class Unit:
    pass


BLOCK = 256


def back_kernel(parts, owners, plan, *refs):
    half = parts // 2
    count = len(plan)
    given = refs[: count - 1]
    slopes, weights, turned, linear, vectors, ratio, replies, picks = refs[count - 1 : count + 7]
    outputs, tokens_out, sums_out = refs[count + 7 : 2 * count + 7], refs[2 * count + 7], refs[2 * count + 8]
    scratch = list(refs[2 * count + 9 :])
    gathered, made, sp, rp, st_, rt_ = scratch[:6]
    ra, rb = scratch[18:20]
    held, stream, stream_sem, grown, gains, shifts, near, far, sn, rn, sf_, rf_ = scratch[6:18]
    scratch = scratch[20:]
    inputs = given + (held,)
    part = lax.axis_index("mdl")
    owner = lax.axis_index("ids")
    low, place = lax.rem(part, 2), part // 2
    pair = {"mdl": part + 1 - 2 * low}
    cross = {"mdl": lax.rem(part + 2, parts)}
    side, row = lax.rem(owner, 2), owner // 2
    twin = {"ids": owner + 1 - 2 * side}
    line = owners // 2
    units = []
    for n, (rows, lanes, chunks, keep, wire) in enumerate(plan):
        bufs = {name: scratch.pop(0) for name in NAMES[: 17 if keep else 13]}
        for c in range(chunks):
            u = Unit()
            u.__dict__.update(bufs)
            u.rows, u.lanes, u.width, u.keep, u.c, u.wire = rows, lanes, lanes // chunks, keep, c, wire
            u.piece = rows // owners
            u.cols = pl.ds(c * u.width, u.width)
            u.source, u.out = inputs[n], outputs[n]
            u.here = n == count - 1
            u.after = None
            units.append(u)
    for u, v in zip(units, units[2:]):
        if u.own is v.own and u.own is not None:
            u.after = v
    greet([gap("mdl", parts, d) for d in range(1, parts)] + [gap("ids", owners, d) for d in range(1, owners)])

    def taken(u, k):
        if not u.here:
            return u.source.at[k, :, u.cols]
        start = pl.multiple_of(k * u.lanes + u.c * u.width, u.width)
        return u.source.at[:, pl.ds(start, u.width)]

    def fetch(u):
        u.mine = [
            pltpu.make_async_copy(taken(u, low + 2 * i), u.own.at[u.c % 2, i], u.sl.at[u.c, i])
            for i in range(half)
        ]
        for copy in u.mine:
            copy.start()

    def begin(u):
        u.first = [
            push(
                taken(u, 1 - low + 2 * i),
                u.got.at[i, :, u.cols],
                u.s0.at[u.c, i],
                u.r0.at[u.c, i],
                pair,
            )
            for i in range(half)
        ]
        for copy in u.first:
            copy.start()

    def sweep(u, body):
        step = min(u.rows, 64)
        blocks(u.rows, step, lambda k: body(pl.ds(k, step)))

    def own_part(u, i, at):
        if u.here:
            start = pl.multiple_of((low + 2 * i) * u.lanes + u.c * u.width, u.width)
            return u.source[at, pl.ds(start, u.width)]
        return u.own[u.c % 2, i, at]

    def to_cross(u):
        for copy in u.first + ([] if u.here else u.mine):
            copy.wait()

        def body(at):
            away = own_part(u, 1 - place, at) + u.got[1 - place, at, u.cols]
            u.out_y[at, u.cols] = away.astype(u.wire)
            u.got[place, at, u.cols] = own_part(u, place, at) + u.got[place, at, u.cols]

        sweep(u, body)
        if u.after is not None:
            fetch(u.after)
        u.second = push(
            u.out_y.at[:, u.cols], u.in_y.at[:, u.cols], u.sy.at[u.c], u.ry.at[u.c], cross
        )
        u.second.start()

    def to_owners(u):
        u.second.wait()

        def body(at):
            value = u.got[place, at, u.cols] + u.in_y[at, u.cols].astype(jnp.float32)
            u.got[place, at, u.cols] = value
            u.out_f[at, u.cols] = value.astype(u.wire)

        sweep(u, body)
        u.third = []
        for d in range(1, owners):
            peer = lax.rem(owner + d, owners)
            copy = push(
                u.out_f.at[pl.ds(pl.multiple_of(peer * u.piece, u.piece), u.piece), u.cols],
                u.in_f.at[d, :, u.cols],
                u.sf.at[u.c, d],
                u.rf.at[u.c, d],
                {"ids": peer},
            )
            copy.start()
            u.third.append(copy)

    def finish(u):
        for copy in u.third:
            copy.wait()
        here = pl.ds(pl.multiple_of(owner * u.piece, u.piece), u.piece)
        value = u.got[place, here, u.cols]
        for d in range(1, owners):
            value = value + u.in_f[d, :, u.cols].astype(jnp.float32)
        if not u.keep:
            u.out[:, u.cols] = value
            return
        u.out[row, side, :, u.cols] = value
        u.fourth = []
        spot = u.out.at[row, side, :, u.cols]
        for d in range(1, line):
            peer = {"ids": lax.rem(row + d, line) * 2 + side}
            copy = push(spot, spot, u.sg.at[u.c, d], u.rg.at[u.c, d], peer)
            copy.start()
            u.fourth.append(copy)

    def to_twin(u):
        if not u.keep:
            return
        for d, copy in zip(range(1, line), u.fourth):
            copy.wait_send()
            there = u.out.at[lax.rem(row + line - d, line), side, :, u.cols]
            push(there, there, u.sg.at[u.c, d], u.rg.at[u.c, d], twin).wait_recv()
        spot = u.out.at[:, side, :, u.cols]
        u.fifth = push(spot, spot, u.st.at[u.c], u.rt.at[u.c], twin)
        u.fifth.start()

    def close(u):
        if not u.keep:
            return
        u.fifth.wait_send()
        there = u.out.at[:, 1 - side, :, u.cols]
        push(there, there, u.st.at[u.c], u.rt.at[u.c], twin).wait_recv()

    rows, hidden = slopes.shape
    bands = hidden // BLOCK
    step = 64

    def band(k):
        return pl.ds(pl.multiple_of(k * BLOCK, BLOCK), BLOCK)

    def load(k, slot):
        return pltpu.make_async_copy(linear.at[:, band(k)], stream.at[slot], stream_sem.at[slot])

    def unit_rows(values, k):
        mean, scale = vectors[0:1, band(k)], vectors[1:2, band(k)]
        return (mish(values) - mean) * scale

    def incoming(k, slot):
        load(k, slot).wait()

        def multiply(r):
            at = pl.ds(r, rows // 2)
            held[at, band(k)] = jnp.dot(
                slopes[at, :], weights[:, band(k)], preferred_element_type=jnp.float32
            )

        blocks(rows, rows // 2, multiply)

        def body(n, sums):
            at = pl.ds(pl.multiple_of(n * step, step), step)
            value = held[at, band(k)]
            product = value * unit_rows(stream[slot, at, :], k)
            return (
                sums[0] + jnp.sum(product.reshape(step // 8, 8, BLOCK), 0),
                sums[1] + jnp.sum(value.reshape(step // 8, 8, BLOCK), 0),
            )

        zero = jnp.zeros((8, BLOCK), jnp.float32)
        gain, shift = lax.fori_loop(0, rows // step, body, (zero, zero))
        gains[0:1, band(k)] = jnp.sum(gain, 0, keepdims=True)
        shifts[0:1, band(k)] = jnp.sum(shift, 0, keepdims=True)

    def outgoing(k, slot):
        load(k, slot).wait()

        def body(n, none):
            at = pl.ds(pl.multiple_of(n * step, step), step)
            values = stream[slot, at, :]
            scale, gain = vectors[1:2, band(k)], vectors[2:3, band(k)]
            pull = shifts[0:1, band(k)] + unit_rows(values, k) * gains[0:1, band(k)]
            back = scale * (gain * held[at, band(k)] - ratio[at, :] * gain * pull)
            grown[at, :] = (mish_slope(values) * back).astype(jnp.bfloat16)
            return none

        lax.fori_loop(0, rows // step, body, 0)

        def multiply(r):
            at = pl.ds(r, rows // 2)
            held[at, band(k)] = jnp.dot(turned[at, :], grown[...], preferred_element_type=jnp.float32)

        blocks(rows, rows // 2, multiply)

    def bands_of(work, order):
        def body(n, none):
            for slot in range(2):
                k = 2 * n + slot

                @pl.when(k + 1 < bands)
                def _():
                    load(order(k + 1), 1 - slot).start()

                work(order(k), slot)
            return none

        return body

    def exchange_sums(meanwhile):
        lines = hidden // 128
        for n in range(lines):
            at = slice(128 * n, 128 * (n + 1))
            near[0, n : n + 1, :] = gains[0:1, at]
            near[0, lines + n : lines + n + 1, :] = shifts[0:1, at]
        copies = [
            push(near.at[0], near.at[d], sn.at[d], rn.at[d], gap("mdl", parts, d))
            for d in range(1, parts)
        ]
        for copy in copies:
            copy.start()
        meanwhile()
        for copy in copies:
            copy.wait()
        total = near[part]
        for k in range(1, parts):
            total = total + near[lax.rem(part + parts - k, parts)]
        far[0] = total
        copies = [
            push(far.at[0], far.at[d], sf_.at[d], rf_.at[d], gap("ids", owners, d))
            for d in range(1, owners)
        ]
        for copy in copies:
            copy.start()
        for copy in copies:
            copy.wait()
        total = far[owner]
        for k in range(1, owners):
            total = total + far[lax.rem(owner + owners - k, owners)]
        sums_out[...] = total
        for n in range(lines):
            at = slice(128 * n, 128 * (n + 1))
            gains[0:1, at] = total[n : n + 1]
            shifts[0:1, at] = total[lines + n : lines + n + 1]

    def share(source, target, send, recv):
        copies = [
            push(source, target.at[part], send.at[d], recv.at[d], gap("mdl", parts, d))
            for d in range(1, parts)
        ]
        for copy in copies:
            copy.start()
        return copies

    piece = replies.shape[2]
    slots = piece * parts

    def select(q):
        def body(j, summed):
            first = j * slots + q * piece
            place_ = lax.broadcasted_iota(jnp.int32, (piece, picks.shape[1]), 0) + first
            chosen = jnp.where(place_ == picks[...], 1.0, 0.0).astype(jnp.bfloat16)
            return summed + jnp.dot(gathered[q, j], chosen, preferred_element_type=jnp.float32)

        start = jnp.zeros((replies.shape[1], picks.shape[1]), jnp.float32)
        summed = lax.fori_loop(0, owners, body, start)
        made[...] = summed.astype(jnp.bfloat16) if q == 0 else made[...] + summed.astype(jnp.bfloat16)

    asked = []
    for d in range(1, owners):
        peer = gap("ids", owners, d)
        copy = push(replies.at[peer["ids"]], gathered.at[part, owner], ra.at[d], rb.at[d], peer)
        copy.start()
        asked.append(copy)
    gathered[part, owner] = replies[owner]
    whole = [u for u in units if not u.here]
    own = [u for u in units if u.here]
    for u in whole:
        begin(u)
    for n, u in enumerate(whole):
        if n == 0 or u.c < 2:
            fetch(u)
    plain = bands_of(incoming, lambda k: k)
    load(0, 0).start()
    per = bands // parts
    spread = bands_of(outgoing, lambda k: lax.rem(k, parts) * per + k // parts)
    total = len(units)
    stages = (to_cross, to_owners, finish, to_twin, close)
    ready = [0]

    def advance():
        t = ready[0]
        ready[0] += 1
        for s, stage in enumerate(stages):
            if 0 <= t - s < total:
                stage(units[t - s])

    loops = bands // 2
    lax.fori_loop(0, loops // 2, plain, 0)
    advance()
    lax.fori_loop(loops // 2, loops, plain, 0)
    exchange_sums(advance)
    advance()
    for copy in asked:
        copy.wait()
    early = share(gathered.at[part], gathered, sp, rp)
    load(0, 0).start()
    for n in range(loops):
        spread(n, 0)
        if (n + 1) % (loops // per) == 0:
            begin(own[(n + 1) * per // loops - 1])
        advance()
    for copy in early:
        copy.wait()
    for q in range(parts):
        advance()
        select(q)
    tokens_out[part] = made[...]
    late = share(made, tokens_out, st_, rt_)
    while ready[0] < total + len(stages) - 1:
        advance()
    for copy in late:
        copy.wait()


def back(arrays, plan, operands, replies, picks, call):
    parts, owners = lax.axis_size("mdl"), lax.axis_size("ids")
    half = parts // 2
    slopes, weights, turned, linear, vectors, ratio = operands
    size, hidden = slopes.shape
    inputs = turned.shape[0]
    assert inputs == size
    found_shape = (replies.shape[1], picks.shape[1])
    dma = pltpu.SemaphoreType.DMA
    lines = 2 * hidden // 128
    outs = []
    scratch = [
        pltpu.VMEM((parts,) + replies.shape, replies.dtype),
        pltpu.VMEM(found_shape, replies.dtype),
    ] + [dma((parts,))] * 4
    scratch += [
        pltpu.VMEM((inputs, hidden), jnp.float32),
        pltpu.VMEM((2, size, BLOCK), jnp.float32),
        dma((2,)),
        pltpu.VMEM((size, BLOCK), jnp.bfloat16),
        pltpu.VMEM((8, hidden), jnp.float32),
        pltpu.VMEM((8, hidden), jnp.float32),
        pltpu.VMEM((parts, lines, 128), jnp.float32),
        pltpu.VMEM((owners, lines, 128), jnp.float32),
        dma((parts,)),
        dma((parts,)),
        dma((owners,)),
        dma((owners,)),
        dma((owners,)),
        dma((owners,)),
    ]
    for rows, lanes, chunks, keep, wire in plan:
        piece = rows // owners
        outs.append(
            jax.ShapeDtypeStruct(
                (owners // 2, 2, piece, lanes) if keep else (piece, lanes), jnp.float32
            )
        )
        scratch += [
            pltpu.VMEM((2, half, rows, lanes // chunks) if keep else (8, 128), jnp.float32),
            pltpu.VMEM((half, rows, lanes), jnp.float32),
            pltpu.VMEM((rows, lanes), wire),
            pltpu.VMEM((rows, lanes), wire),
            pltpu.VMEM((rows, lanes), wire),
            pltpu.VMEM((owners, piece, lanes), wire),
            dma((chunks, half)),
            dma((chunks, half)),
            dma((chunks, half)),
            dma((chunks,)),
            dma((chunks,)),
            dma((chunks, owners)),
            dma((chunks, owners)),
        ]
        if keep:
            scratch += [
                dma((chunks, owners // 2)),
                dma((chunks, owners // 2)),
                dma((chunks,)),
                dma((chunks,)),
            ]
    held = pl.BlockSpec(memory_space=pl.ANY)
    whole = pl.BlockSpec(memory_space=pltpu.VMEM)
    found = pl.pallas_call(
        functools.partial(back_kernel, parts, owners, plan),
        out_shape=tuple(outs)
        + (
            jax.ShapeDtypeStruct((parts,) + found_shape, replies.dtype),
            jax.ShapeDtypeStruct((lines, 128), jnp.float32),
        ),
        in_specs=[held] * len(arrays) + [whole, whole, whole, held, whole, whole] + [whole] * 2,
        out_specs=(whole,) * (len(plan) + 2),
        scratch_shapes=scratch,
        compiler_params=pltpu.CompilerParams(
            collective_id=call, has_side_effects=True, vmem_limit_bytes=67043328
        ),
        name="back",
    )(*arrays, *operands, replies, picks)
    grads = tuple(v.reshape(-1, v.shape[-1]) for v in found[: len(plan)])
    return grads + (found[-2], found[-1].reshape(2, hidden))


def total(vectors, small, extras, kinds, call):
    rows = [v.reshape(-1, LANES) for v in vectors]
    sizes = [r.shape[0] for r in rows]
    if small is not None:
        rows.append(jnp.pad(small.reshape(1, -1), ((0, 7), (0, LANES - small.size))))
    summed, *moved = exchange(jnp.concatenate(rows, axis=0), extras, kinds, call)
    found, start = [], 0
    for size in sizes:
        found.append(summed[start : start + size].reshape(-1))
        start += size
    if small is not None:
        found.append(summed[start, : small.size])
    return found, moved


def body(
    hash_codes,
    request_ids,
    request_counts,
    token_slots,
    cotangent,
    weight_first,
    weight_second,
    weight_final,
    norm_params,
    bias_final,
    moment_first,
    square_first,
    moment_second,
    square_second,
    moment_final,
    square_final,
    moment_norm,
    square_norm,
    moment_bias,
    square_bias,
):
    owners = lax.axis_size("ids")
    parts = lax.axis_size("mdl")
    part = lax.axis_index("mdl")
    range_rows = hash_codes.shape[0]
    rows = range_rows // parts
    slots_per = request_ids.shape[1]
    piece = slots_per // parts
    out_width = weight_final.shape[1]
    width = weight_first.shape[1]
    wide = width + (-width) % LANES
    hidden = wide * parts
    more = wide - width
    token_count = token_slots.shape[0]
    token_piece = token_count // parts
    token_total = token_count * owners

    encoded = ((hash_codes.astype(jnp.float32) + 0.5) / 512.0 - 1.0).astype(jnp.bfloat16)
    owner_row = jnp.arange(owners, dtype=jnp.int32)[:, None]
    wanted = jnp.where(
        jnp.arange(slots_per, dtype=jnp.int32)[None, :] < request_counts[:, None],
        request_ids - owner_row * range_rows,
        range_rows,
    )
    first_low, features, norm_all, final_all, received = front(
        jnp.pad(weight_first.astype(jnp.bfloat16), ((0, 0), (0, more))),
        encoded.reshape(parts, rows, -1),
        jnp.pad(norm_params, ((0, 4), (0, more))),
        jnp.pad(weight_final.astype(jnp.bfloat16).T, ((0, 0), (0, more))),
        wanted.reshape(owners, 1, slots_per),
        5,
    )
    norm_all = norm_all.transpose(1, 0, 2).reshape(-1, hidden)[:4]
    final_low = final_all.transpose(1, 0, 2).reshape(out_width, hidden)
    second_part = jnp.pad(
        weight_second.T.astype(jnp.bfloat16).reshape(width, parts, width),
        ((0, more), (0, 0), (0, more)),
    ).reshape(wide, hidden)
    second_part, first_low = lax.optimization_barrier((second_part, first_low))
    second_low = lax.all_gather(second_part, "mdl", axis=0, tiled=True)

    received = received.reshape(owners, slots_per)
    here = part * rows + jnp.arange(rows, dtype=jnp.int32)
    live_mask = jnp.max(
        (received.reshape(1, -1) == here[:, None]).astype(jnp.float32), axis=1
    )
    slots_mine = lax.dynamic_slice(received, (0, part * piece), (owners, piece)).reshape(-1)
    pick_rows = (
        slots_mine[:, None] == lax.broadcasted_iota(jnp.int32, (owners * piece, range_rows), 1)
    ).astype(jnp.bfloat16)

    slot_owner = token_slots // slots_per
    slot_place = token_slots % slots_per - part * piece
    slot_here = jnp.where(
        (slot_place >= 0) & (slot_place < piece), slot_owner * piece + slot_place, -1
    )
    slot_sum = contract(cotangent, one_hot(slot_here, owners * piece, 0), 0, 1) / token_total
    sent = jnp.concatenate(split_two(slot_sum), axis=0)
    sent = sent.reshape(2 * out_width, owners, piece).transpose(1, 0, 2)

    linear_one = jnp.dot(features, first_low, preferred_element_type=jnp.float32)
    active_one = mish(linear_one)
    weighted_one = live_mask[:, None] * active_one
    (*sums_one, live_count), (arrived,) = total(
        [jnp.sum(weighted_one, 0), jnp.sum(weighted_one * active_one, 0)],
        jnp.sum(live_mask).reshape(1),
        [sent],
        (("ids", True),),
        0,
    )
    live_count = live_count[0]
    mean_one = sums_one[0] / live_count
    scale_one = lax.rsqrt(sums_one[1] / live_count - mean_one * mean_one + norm_epsilon)
    unit_one = (active_one - mean_one) * scale_one
    normed_one = (norm_all[0] * unit_one + norm_all[1]).astype(jnp.bfloat16)
    arrived = arrived.transpose(1, 0, 2).reshape(2 * out_width, owners * piece)
    row_part = jnp.dot(arrived, pick_rows, preferred_element_type=jnp.float32)
    row_part = (row_part[:out_width] + row_part[out_width:]).reshape(out_width, parts, rows)
    linear_two = contract(normed_one, second_low, 1, 1)
    active_two = mish(linear_two)
    weighted_two = live_mask[:, None] * active_two
    sums_two, (row_parts,) = total(
        [jnp.sum(weighted_two, 0), jnp.sum(weighted_two * active_two, 0)],
        None,
        [row_part.transpose(1, 0, 2)],
        (("mdl", True),),
        1,
    )
    row_grad = jnp.sum(row_parts, 0)
    mean_two = sums_two[0] / live_count
    scale_two = lax.rsqrt(sums_two[1] / live_count - mean_two * mean_two + norm_epsilon)
    unit_two = (active_two - mean_two) * scale_two
    normed_two = (norm_all[2] * unit_two + norm_all[3]).astype(jnp.bfloat16)
    embedding = contract(final_low, normed_two, 1, 1) + bias_final[:, None]

    grad_embed = (
        row_grad + 2.0 * penalty_weight / live_count * live_mask[None, :] * embedding
    ).astype(jnp.bfloat16)
    incoming_two = contract(grad_embed, final_low, 0, 0)
    (*sums_two, grad_bias), (embed_range,) = total(
        [jnp.sum(incoming_two * unit_two, 0), jnp.sum(incoming_two, 0)],
        jnp.sum(grad_embed.astype(jnp.float32), 1),
        [embedding.astype(jnp.bfloat16)],
        (("mdl", False),),
        2,
    )
    embed_range = embed_range.transpose(1, 0, 2).reshape(out_width, range_rows)
    replies = contract(embed_range, pick_rows, 1, 1).astype(jnp.bfloat16)
    replies = replies.reshape(out_width, owners, piece).transpose(1, 0, 2)
    local_final = jnp.pad(
        contract(normed_two, grad_embed, 0, 1).reshape(parts, wide, out_width),
        ((0, 0), (0, 0), (0, (-out_width) % LANES)),
    )
    outgoing_two = norm_back(
        incoming_two, unit_two, norm_all[2], scale_two, live_mask, sums_two[0], sums_two[1], live_count
    )
    grad_linear_two = (mish_slope(linear_two) * outgoing_two).astype(jnp.bfloat16)
    local_second = contract(grad_linear_two, normed_one, 0, 0).reshape(parts, wide, hidden)
    tokens_mine = lax.dynamic_slice(token_slots, (part * token_piece,), (token_piece,))
    second_sum, final_sum, first_sum, tokens, sums_one = back(
        (local_second, local_final),
        (
            (wide, hidden, 8, True, jnp.bfloat16),
            (wide, local_final.shape[2], 1, True, jnp.float32),
            (features.shape[1], wide, wide // BLOCK, False, jnp.bfloat16),
        ),
        (
            grad_linear_two,
            second_low,
            features.T,
            linear_one,
            jnp.pad(jnp.stack([mean_one, scale_one, norm_all[0]]), ((0, 5), (0, 0))),
            (live_mask / live_count)[:, None],
        ),
        replies,
        tokens_mine.reshape(1, token_piece),
        4,
    )
    token_embed = tokens.transpose(0, 2, 1).reshape(token_count, out_width)
    grad_second = second_sum[:width].reshape(width, parts, wide)
    grad_second = grad_second[:, :, :width].reshape(width, parts * width).T
    grad_final = final_sum[:width, :out_width]
    grad_first = first_sum[:, :width]
    start = part * wide
    grad_norm = lax.dynamic_slice(jnp.stack([*sums_one, *sums_two]), (0, start), (4, width))
    momentum_first, variance_first, master_first = adam(
        weight_first, moment_first, square_first, grad_first, rate_matrix, decay_matrix
    )
    momentum_second, variance_second, master_second = adam(
        weight_second, moment_second, square_second, grad_second, rate_matrix, decay_matrix
    )
    momentum_final, variance_final, master_final = adam(
        weight_final, moment_final, square_final, grad_final, rate_matrix, decay_matrix
    )
    momentum_norm, variance_norm, master_norm = adam(
        norm_params, moment_norm, square_norm, grad_norm, rate_norm, 0.0
    )
    momentum_bias, variance_bias, master_bias = adam(
        bias_final, moment_bias, square_bias, grad_bias, rate_bias, 0.0
    )
    return (
        token_embed,
        momentum_first,
        variance_first,
        master_first,
        master_first.astype(jnp.bfloat16),
        momentum_second,
        variance_second,
        master_second,
        master_second.astype(jnp.bfloat16),
        momentum_final,
        variance_final,
        master_final,
        master_final.astype(jnp.bfloat16),
        momentum_norm,
        variance_norm,
        master_norm,
        momentum_bias,
        variance_bias,
        master_bias,
    )


def solution(mesh):
    rows = P("ids", None)
    grid = P("ids", "mdl")
    columns = P(None, "mdl")
    mdl_rows = P("mdl", None)
    return jax.shard_map(
        body,
        mesh=mesh,
        in_specs=(grid, rows, P("ids"), P("ids"), rows, grid, columns, mdl_rows, columns, P())
        + (grid,) * 2
        + (columns,) * 2
        + (mdl_rows,) * 2
        + (columns,) * 2
        + (P(),) * 2,
        out_specs=(rows,)
        + (grid,) * 4
        + (columns,) * 4
        + (mdl_rows,) * 4
        + (columns,) * 3
        + (P(),) * 3,
        check_vma=False,
    )
```

```python
import functools
import jax
import jax.numpy as jnp
from jax import lax
from jax.experimental import pallas as pl
from jax.experimental.pallas import tpu as pltpu
from jax.sharding import PartitionSpec as P

STEP = 10


beta_one = 0.9
beta_two = 0.999
adam_epsilon = 1e-08
norm_epsilon = 1e-05
penalty_weight = 0.25
decay_matrix = 0.01
rate_matrix = 0.05
rate_norm = 0.5
rate_bias = 0.02
LANES = 128


def mish_parts(inputs):
    grown = jnp.exp(jnp.minimum(inputs, 20.0))
    above = grown * (grown + 2.0)
    inverse = 1.0 / (above + 2.0)
    return grown, above * inverse, inverse


def mish(inputs):
    return inputs * mish_parts(inputs)[1]


def mish_slope(inputs):
    grown, gate, inverse = mish_parts(inputs)
    return gate + 4.0 * jnp.minimum(inputs, 20.0) * (grown * inverse) * ((1.0 + grown) * inverse)


def contract(left, right, left_dim, right_dim):
    return lax.dot_general(
        left, right, (((left_dim,), (right_dim,)), ((), ())), preferred_element_type=jnp.float32
    )


def norm_back(upstream, unit_rows, gain_row, scale_row, live_mask, gain_sum, shift_sum, live_count):
    return scale_row * (
        gain_row * upstream
        - live_mask[:, None] * gain_row * (shift_sum + unit_rows * gain_sum) / live_count
    )


def adam(weight, moment, square, gradient, step_rate, shrink):
    momentum = beta_one * moment + (1.0 - beta_one) * gradient
    variance = beta_two * square + (1.0 - beta_two) * gradient * gradient
    moment_hat = momentum / (1.0 - beta_one**STEP)
    square_hat = variance / (1.0 - beta_two**STEP)
    master = weight - step_rate * (
        moment_hat / (jnp.sqrt(square_hat) + adam_epsilon) + shrink * weight
    )
    return (momentum, variance, master)


def split_two(values):
    high = values.astype(jnp.bfloat16)
    low = (values - high.astype(jnp.float32)).astype(jnp.bfloat16)
    return high, low


def one_hot(index, length, first):
    rows = lax.broadcasted_iota(jnp.int32, (length, index.shape[0]), 0) + first
    return (rows == index[None, :]).astype(jnp.bfloat16)


MESH = pl.DeviceIdType.MESH
BLOCK = 256


def greet(peers):
    barrier = pltpu.get_barrier_semaphore()
    for peer in peers:
        pl.semaphore_signal(barrier, inc=1, device_id=peer, device_id_type=MESH)
    pl.semaphore_wait(barrier, len(peers))


def push(source, target, send_sem, recv_sem, peer):
    return pltpu.make_async_remote_copy(
        src_ref=source,
        dst_ref=target,
        send_sem=send_sem,
        recv_sem=recv_sem,
        device_id=peer,
        device_id_type=MESH,
    )


def gap(axis, size, d):
    return {axis: lax.rem(lax.axis_index(axis) + d, size)}


def exchange_kernel(parts, owners, kinds, *refs):
    extras = len(kinds)
    x_ref, given = refs[0], refs[1 : 1 + extras]
    o_ref, taken = refs[1 + extras], refs[2 + extras : 2 + 2 * extras]
    near, far, send_near, recv_near, send_far, recv_far, *sems = refs[2 + 2 * extras :]
    sizes = {"mdl": parts, "ids": owners}
    part = lax.axis_index("mdl")
    owner = lax.axis_index("ids")
    greet([gap("mdl", parts, d) for d in range(1, parts)] + [gap("ids", owners, d) for d in range(1, owners)])
    copies = [
        push(x_ref, near.at[d], send_near.at[d], recv_near.at[d], gap("mdl", parts, d))
        for d in range(1, parts)
    ]
    for copy in copies:
        copy.start()
    others = []
    for n, (axis, spread) in enumerate(kinds):
        me = lax.axis_index(axis)
        for d in range(1, sizes[axis]):
            peer = gap(axis, sizes[axis], d)
            source = given[n].at[peer[axis]] if spread else given[n]
            copy = push(source, taken[n].at[me], sems[2 * n].at[d], sems[2 * n + 1].at[d], peer)
            copy.start()
            others.append(copy)
        taken[n][me] = given[n][me] if spread else given[n][...]
    near[0] = x_ref[...]
    for copy in copies:
        copy.wait()
    total = near[part]
    for k in range(1, parts):
        total = total + near[lax.rem(part + parts - k, parts)]
    far[0] = total
    copies = [
        push(far.at[0], far.at[d], send_far.at[d], recv_far.at[d], gap("ids", owners, d))
        for d in range(1, owners)
    ]
    for copy in copies:
        copy.start()
    for copy in copies:
        copy.wait()
    total = far[owner]
    for k in range(1, owners):
        total = total + far[lax.rem(owner + owners - k, owners)]
    o_ref[...] = total
    for copy in others:
        copy.wait()


def exchange(x, extras, kinds, call):
    parts, owners = lax.axis_size("mdl"), lax.axis_size("ids")
    sizes = {"mdl": parts, "ids": owners}
    dma = pltpu.SemaphoreType.DMA
    whole = pl.BlockSpec(memory_space=pltpu.VMEM)
    outs = [jax.ShapeDtypeStruct(x.shape, jnp.float32)]
    sems = []
    for extra, (axis, spread) in zip(extras, kinds):
        shape = extra.shape if spread else (sizes[axis],) + extra.shape
        outs.append(jax.ShapeDtypeStruct(shape, extra.dtype))
        sems += [dma((sizes[axis],)), dma((sizes[axis],))]
    return pl.pallas_call(
        functools.partial(exchange_kernel, parts, owners, kinds),
        out_shape=tuple(outs),
        in_specs=[whole] * (1 + len(extras)),
        out_specs=(whole,) * len(outs),
        scratch_shapes=[
            pltpu.VMEM((parts,) + x.shape, jnp.float32),
            pltpu.VMEM((owners,) + x.shape, jnp.float32),
            dma((parts,)),
            dma((parts,)),
            dma((owners,)),
            dma((owners,)),
        ]
        + sems,
        compiler_params=pltpu.CompilerParams(collective_id=call, has_side_effects=True),
        name="exchange",
    )(x, *extras)


def front_kernel(
    parts, owners, first, codes, norms, final, wanted, places, pulls,
    weights, feats, norms_all, final_all, received, slot_sums,
    s1, r1, s2, r2, s3, r3, sc, rc, sn, rn, sw, rw, sl,
):
    part = lax.axis_index("mdl")
    owner = lax.axis_index("ids")
    pair = {"mdl": part + 1 - 2 * lax.rem(part, 2)}
    cross_part = lax.rem(part + 2, parts)
    cross = {"mdl": cross_part}
    rows, width = first.shape
    codes_width = codes.shape[2]
    greet([gap("mdl", parts, d) for d in range(1, parts)] + [gap("ids", owners, d) for d in range(1, owners)])

    def spot(who, which):
        return weights.at[
            pl.ds(pl.multiple_of(who * rows, rows), rows),
            pl.ds(pl.multiple_of(which * width, width), width),
        ]

    mine = feats.at[:, pl.ds(pl.multiple_of(part * codes_width, codes_width), codes_width)]
    locals_ = [
        pltpu.make_async_copy(first, spot(owner, part), sl.at[0]),
        pltpu.make_async_copy(codes.at[part], mine, sl.at[1]),
    ]
    for copy in locals_:
        copy.start()
    ones, lines = [], []
    for d in range(1, owners):
        peer = gap("ids", owners, d)
        copy = push(first, spot(owner, part), s1.at[d], r1.at[d], peer)
        copy.start()
        ones.append(copy)
        copy = push(wanted.at[peer["ids"]], received.at[owner], sw.at[d], rw.at[d], peer)
        copy.start()
        lines.append(copy)
    for d in range(1, parts):
        peer = gap("mdl", parts, d)
        for n, (source, target) in enumerate(((norms, norms_all), (final, final_all))):
            copy = push(source, target.at[part], sn.at[n, d], rn.at[n, d], peer)
            copy.start()
            lines.append(copy)
    for d in range(1, parts):
        peer = gap("mdl", parts, d)
        copy = push(codes.at[peer["mdl"]], mine, sc.at[d], rc.at[d], peer)
        copy.start()
        lines.append(copy)
    received[owner] = wanted[owner]
    norms_all[part] = norms[...]
    final_all[part] = final[...]
    tokens, slots = places.shape[1], slot_sums.shape[1]
    run = min(tokens, 1024)
    runs = tokens // run

    def gather_slots(start, stop):
        def one(n, none):
            at = pl.ds(pl.multiple_of(n * BLOCK, BLOCK), BLOCK)

            def body(k, summed):
                cols = pl.ds(pl.multiple_of(k * run, run), run)
                which = lax.broadcasted_iota(jnp.int32, (BLOCK, run), 0) + n * BLOCK
                here = jnp.where(which == places[0:1, cols], 1.0, 0.0).astype(jnp.bfloat16)
                return summed + contract(pulls[:, cols], here, 1, 1)

            slot_sums[:, at] = lax.fori_loop(
                0, runs, body, jnp.zeros((pulls.shape[0], BLOCK), jnp.float32)
            )
            return none

        lax.fori_loop(start, stop, one, 0)

    count = slots // BLOCK
    gather_slots(0, count // 2)
    twos, threes = [], []
    for d in range(owners):
        who = lax.rem(owner + owners - d, owners)
        if d == 0:
            locals_[0].wait()
        else:
            ones[d - 1].wait_send()
            push(first, spot(who, part), s1.at[d], r1.at[d], pair).wait_recv()
        piece = spot(who, part)
        copy = push(piece, piece, s2.at[d], r2.at[d], cross)
        copy.start()
        twos.append(copy)
        copy = push(piece, piece, s3.at[0, d], r3.at[0, d], pair)
        copy.start()
        threes.append(copy)
    gather_slots(count // 2, count)
    for d in range(owners):
        who = lax.rem(owner + owners - d, owners)
        twos[d].wait_send()
        piece = spot(who, cross_part)
        push(piece, piece, s2.at[d], r2.at[d], cross).wait_recv()
        copy = push(piece, piece, s3.at[1, d], r3.at[1, d], pair)
        copy.start()
        threes.append(copy)
    for copy in threes + lines:
        copy.wait()
    locals_[1].wait()


def front(first, codes, norms, final, wanted, places, pulls, slots, call):
    parts, owners = lax.axis_size("mdl"), lax.axis_size("ids")
    dma = pltpu.SemaphoreType.DMA
    held = pl.BlockSpec(memory_space=pl.ANY)
    whole = pl.BlockSpec(memory_space=pltpu.VMEM)
    shape = jax.ShapeDtypeStruct
    return pl.pallas_call(
        functools.partial(front_kernel, parts, owners),
        out_shape=(
            shape((first.shape[0] * owners, first.shape[1] * parts), first.dtype),
            shape((codes.shape[1], codes.shape[2] * parts), codes.dtype),
            shape((parts,) + norms.shape, norms.dtype),
            shape((parts,) + final.shape, final.dtype),
            shape(wanted.shape, wanted.dtype),
            shape((pulls.shape[0], slots), jnp.float32),
        ),
        in_specs=[whole] * 7,
        out_specs=(held, held, whole, whole, whole, whole),
        scratch_shapes=[dma((owners,))] * 4
        + [dma((2, owners))] * 2
        + [dma((parts,))] * 2
        + [dma((2, parts))] * 2
        + [dma((owners,))] * 2
        + [dma((2,))],
        compiler_params=pltpu.CompilerParams(collective_id=call, has_side_effects=True, vmem_limit_bytes=16 * 1024 * 1024),
        name="front",
    )(first, codes, norms, final, wanted, places, pulls)


def blocks(count, step, body):
    if count == step:
        body(0)
    else:
        @pl.loop(0, count // step)
        def _(k):
            body(pl.multiple_of(k * step, step))


NAMES = (
    "own",
    "got",
    "out_y",
    "in_y",
    "out_f",
    "in_f",
    "s0",
    "r0",
    "sl",
    "sy",
    "ry",
    "sf",
    "rf",
    "sg",
    "rg",
    "st",
    "rt",
)


class Unit:
    pass


def back_kernel(parts, owners, plan, *refs):
    half = parts // 2
    count = len(plan)
    given = refs[: count - 1]
    slopes, weights, turned, linear, vectors, ratio, replies, picks, lasts = refs[count - 1 : count + 8]
    outputs, tokens_out, sums_out = refs[count + 8 : 2 * count + 8], refs[2 * count + 8], refs[2 * count + 9]
    last_out = refs[2 * count + 10]
    scratch = list(refs[2 * count + 11 :])
    last_in, last_sum, last_far, l1, l2, l3, l4, l5, l6 = scratch[:9]
    scratch = scratch[9:]
    gathered, made, sp, rp, st_, rt_ = scratch[:6]
    ra, rb = scratch[18:20]
    held, stream, stream_sem, grown, gains, shifts, near, far, sn, rn, sf_, rf_ = scratch[6:18]
    scratch = scratch[20:]
    inputs = given + (held,)
    part = lax.axis_index("mdl")
    owner = lax.axis_index("ids")
    low, place = lax.rem(part, 2), part // 2
    pair = {"mdl": part + 1 - 2 * low}
    cross = {"mdl": lax.rem(part + 2, parts)}
    side, row = lax.rem(owner, 2), owner // 2
    twin = {"ids": owner + 1 - 2 * side}
    line = owners // 2
    units = []
    for n, (rows, lanes, chunks, keep, wire) in enumerate(plan):
        bufs = {name: scratch.pop(0) for name in NAMES[: 17 if keep else 13]}
        for c in range(chunks):
            u = Unit()
            u.__dict__.update(bufs)
            u.rows, u.lanes, u.width, u.keep, u.c, u.wire = rows, lanes, lanes // chunks, keep, c, wire
            u.piece = rows // owners
            u.cols = pl.ds(c * u.width, u.width)
            u.source, u.out = inputs[n], outputs[n]
            u.here = n == count - 1
            u.after = None
            units.append(u)
    for u, v in zip(units, units[2:]):
        if u.own is v.own and u.own is not None:
            u.after = v
    greet([gap("mdl", parts, d) for d in range(1, parts)] + [gap("ids", owners, d) for d in range(1, owners)])

    def taken(u, k):
        if not u.here:
            return u.source.at[k, :, u.cols]
        start = pl.multiple_of(k * u.lanes + u.c * u.width, u.width)
        return u.source.at[:, pl.ds(start, u.width)]

    def fetch(u):
        u.mine = [
            pltpu.make_async_copy(taken(u, low + 2 * i), u.own.at[u.c % 2, i], u.sl.at[u.c, i])
            for i in range(half)
        ]
        for copy in u.mine:
            copy.start()

    def begin(u):
        u.first = [
            push(
                taken(u, 1 - low + 2 * i),
                u.got.at[i, :, u.cols],
                u.s0.at[u.c, i],
                u.r0.at[u.c, i],
                pair,
            )
            for i in range(half)
        ]
        for copy in u.first:
            copy.start()

    def sweep(u, body):
        step = min(u.rows, 64)
        blocks(u.rows, step, lambda k: body(pl.ds(k, step)))

    def own_part(u, i, at):
        if u.here:
            start = pl.multiple_of((low + 2 * i) * u.lanes + u.c * u.width, u.width)
            return u.source[at, pl.ds(start, u.width)]
        return u.own[u.c % 2, i, at]

    def to_cross(u):
        for copy in u.first + ([] if u.here else u.mine):
            copy.wait()

        def body(at):
            away = own_part(u, 1 - place, at) + u.got[1 - place, at, u.cols]
            u.out_y[at, u.cols] = away.astype(u.wire)
            u.got[place, at, u.cols] = own_part(u, place, at) + u.got[place, at, u.cols]

        sweep(u, body)
        if u.after is not None:
            fetch(u.after)
        u.second = push(
            u.out_y.at[:, u.cols], u.in_y.at[:, u.cols], u.sy.at[u.c], u.ry.at[u.c], cross
        )
        u.second.start()

    def to_owners(u):
        u.second.wait()

        def body(at):
            value = u.got[place, at, u.cols] + u.in_y[at, u.cols].astype(jnp.float32)
            u.got[place, at, u.cols] = value
            u.out_f[at, u.cols] = value.astype(u.wire)

        sweep(u, body)
        u.third = []
        for d in range(1, owners):
            peer = lax.rem(owner + d, owners)
            copy = push(
                u.out_f.at[pl.ds(pl.multiple_of(peer * u.piece, u.piece), u.piece), u.cols],
                u.in_f.at[d, :, u.cols],
                u.sf.at[u.c, d],
                u.rf.at[u.c, d],
                {"ids": peer},
            )
            copy.start()
            u.third.append(copy)

    def finish(u):
        for copy in u.third:
            copy.wait()
        here = pl.ds(pl.multiple_of(owner * u.piece, u.piece), u.piece)
        value = u.got[place, here, u.cols]
        for d in range(1, owners):
            value = value + u.in_f[d, :, u.cols].astype(jnp.float32)
        if not u.keep:
            u.out[u.cols, :] = value.T
            return
        u.out[row, side, :, u.cols] = value
        u.fourth = []
        spot = u.out.at[row, side, :, u.cols]
        for d in range(1, line):
            peer = {"ids": lax.rem(row + d, line) * 2 + side}
            copy = push(spot, spot, u.sg.at[u.c, d], u.rg.at[u.c, d], peer)
            copy.start()
            u.fourth.append(copy)

    def to_twin(u):
        if not u.keep:
            return
        for d, copy in zip(range(1, line), u.fourth):
            copy.wait_send()
            there = u.out.at[lax.rem(row + line - d, line), side, :, u.cols]
            push(there, there, u.sg.at[u.c, d], u.rg.at[u.c, d], twin).wait_recv()
        spot = u.out.at[:, side, :, u.cols]
        u.fifth = push(spot, spot, u.st.at[u.c], u.rt.at[u.c], twin)
        u.fifth.start()

    def close(u):
        if not u.keep:
            return
        u.fifth.wait_send()
        there = u.out.at[:, 1 - side, :, u.cols]
        push(there, there, u.st.at[u.c], u.rt.at[u.c], twin).wait_recv()

    rows, hidden = slopes.shape
    bands = hidden // BLOCK
    step = 64

    def band(k):
        return pl.ds(pl.multiple_of(k * BLOCK, BLOCK), BLOCK)

    def load(k, slot):
        return pltpu.make_async_copy(linear.at[:, band(k)], stream.at[slot], stream_sem.at[slot])

    def unit_rows(values, k):
        mean, scale = vectors[0:1, band(k)], vectors[1:2, band(k)]
        return (mish(values) - mean) * scale

    def incoming(k, slot):
        load(k, slot).wait()

        def multiply(r):
            at = pl.ds(r, rows // 2)
            held[at, band(k)] = jnp.dot(
                slopes[at, :], weights[:, band(k)], preferred_element_type=jnp.float32
            )

        blocks(rows, rows // 2, multiply)

        def body(n, sums):
            at = pl.ds(pl.multiple_of(n * step, step), step)
            value = held[at, band(k)]
            product = value * unit_rows(stream[slot, at, :], k)
            return (
                sums[0] + jnp.sum(product.reshape(step // 8, 8, BLOCK), 0),
                sums[1] + jnp.sum(value.reshape(step // 8, 8, BLOCK), 0),
            )

        zero = jnp.zeros((8, BLOCK), jnp.float32)
        gain, shift = lax.fori_loop(0, rows // step, body, (zero, zero))
        gains[0:1, band(k)] = jnp.sum(gain, 0, keepdims=True)
        shifts[0:1, band(k)] = jnp.sum(shift, 0, keepdims=True)

    def outgoing(k, slot):
        load(k, slot).wait()

        def body(n, none):
            at = pl.ds(pl.multiple_of(n * step, step), step)
            values = stream[slot, at, :]
            scale, gain = vectors[1:2, band(k)], vectors[2:3, band(k)]
            pull = shifts[0:1, band(k)] + unit_rows(values, k) * gains[0:1, band(k)]
            back = scale * (gain * held[at, band(k)] - ratio[at, :] * gain * pull)
            grown[at, :] = (mish_slope(values) * back).astype(jnp.bfloat16)
            return none

        lax.fori_loop(0, rows // step, body, 0)

        def multiply(r):
            at = pl.ds(r, rows // 2)
            held[at, band(k)] = jnp.dot(turned[at, :], grown[...], preferred_element_type=jnp.float32)

        blocks(rows, rows // 2, multiply)

    def bands_of(work, order):
        def body(n, none):
            for slot in range(2):
                k = 2 * n + slot

                @pl.when(k + 1 < bands)
                def _():
                    load(order(k + 1), 1 - slot).start()

                work(order(k), slot)
            return none

        return body

    def exchange_sums(meanwhile):
        lines = hidden // 128
        for n in range(lines):
            at = slice(128 * n, 128 * (n + 1))
            near[0, n : n + 1, :] = gains[0:1, at]
            near[0, lines + n : lines + n + 1, :] = shifts[0:1, at]
        copies = [
            push(near.at[0], near.at[d], sn.at[d], rn.at[d], gap("mdl", parts, d))
            for d in range(1, parts)
        ]
        for copy in copies:
            copy.start()
        meanwhile()
        for copy in copies:
            copy.wait()
        total = near[part]
        for k in range(1, parts):
            total = total + near[lax.rem(part + parts - k, parts)]
        far[0] = total
        copies = [
            push(far.at[0], far.at[d], sf_.at[d], rf_.at[d], gap("ids", owners, d))
            for d in range(1, owners)
        ]
        for copy in copies:
            copy.start()
        for copy in copies:
            copy.wait()
        total = far[owner]
        for k in range(1, owners):
            total = total + far[lax.rem(owner + owners - k, owners)]
        sums_out[...] = total
        for n in range(lines):
            at = slice(128 * n, 128 * (n + 1))
            gains[0:1, at] = total[n : n + 1]
            shifts[0:1, at] = total[lines + n : lines + n + 1]

    def share(source, target, send, recv):
        copies = [
            push(source, target.at[part], send.at[d], recv.at[d], gap("mdl", parts, d))
            for d in range(1, parts)
        ]
        for copy in copies:
            copy.start()
        return copies

    piece = replies.shape[2]
    slots = piece * parts

    def select(q):
        def body(j, summed):
            first = j * slots + q * piece
            place_ = lax.broadcasted_iota(jnp.int32, (piece, picks.shape[1]), 0) + first
            chosen = jnp.where(place_ == picks[...], 1.0, 0.0).astype(jnp.bfloat16)
            return summed + jnp.dot(gathered[q, j], chosen, preferred_element_type=jnp.float32)

        start = jnp.zeros((replies.shape[1], picks.shape[1]), jnp.float32)
        summed = lax.fori_loop(0, owners, body, start)
        made[...] = summed.astype(jnp.bfloat16) if q == 0 else made[...] + summed.astype(jnp.bfloat16)

    asked = []
    for d in range(1, owners):
        peer = gap("ids", owners, d)
        copy = push(replies.at[peer["ids"]], gathered.at[part, owner], ra.at[d], rb.at[d], peer)
        copy.start()
        asked.append(copy)
    gathered[part, owner] = replies[owner]
    last_trips = [
        push(lasts.at[gap("mdl", parts, d)["mdl"]], last_in.at[d], l1.at[d], l2.at[d], gap("mdl", parts, d))
        for d in range(1, parts)
    ]
    for copy in last_trips:
        copy.start()

    def last_to_owners():
        for copy in last_trips:
            copy.wait()
        value = lasts[part]
        for d in range(1, parts):
            value = value + last_in[d]
        last_sum[...] = value
        copies = [
            push(last_sum.at[gap("ids", owners, d)["ids"]], last_far.at[d], l3.at[d], l4.at[d], gap("ids", owners, d))
            for d in range(1, owners)
        ]
        for copy in copies:
            copy.start()
        return copies

    def last_to_all(copies):
        for copy in copies:
            copy.wait()
        value = last_sum[owner]
        for d in range(1, owners):
            value = value + last_far[d]
        last_out[owner] = value
        spot = last_out.at[owner]
        copies = [
            push(spot, spot, l5.at[d], l6.at[d], gap("ids", owners, d)) for d in range(1, owners)
        ]
        for copy in copies:
            copy.start()
        return copies

    whole = [u for u in units if not u.here]
    own = [u for u in units if u.here]
    for u in whole:
        begin(u)
    for n, u in enumerate(whole):
        if n == 0 or u.c < 2:
            fetch(u)
    plain = bands_of(incoming, lambda k: k)
    load(0, 0).start()
    per = bands // parts
    spread = bands_of(outgoing, lambda k: lax.rem(k, parts) * per + k // parts)
    total = len(units)
    stages = (to_cross, to_owners, finish, to_twin, close)
    ready = [0]

    def advance():
        t = ready[0]
        ready[0] += 1
        for s, stage in enumerate(stages):
            if 0 <= t - s < total:
                stage(units[t - s])

    loops = bands // 2
    lax.fori_loop(0, loops // 2, plain, 0)
    advance()
    lax.fori_loop(loops // 2, loops, plain, 0)
    exchange_sums(advance)
    advance()
    for copy in asked:
        copy.wait()
    early = share(gathered.at[part], gathered, sp, rp)
    load(0, 0).start()
    trips = last_to_owners()
    for n in range(loops):
        spread(n, 0)
        if (n + 1) % (loops // per) == 0:
            begin(own[(n + 1) * per // loops - 1])
        advance()
    for copy in early:
        copy.wait()
    trips = last_to_all(trips)
    for q in range(parts):
        advance()
        select(q)
    tokens_out[part] = made[...]
    late = share(made, tokens_out, st_, rt_)
    while ready[0] < total + len(stages) - 1:
        advance()
    for copy in late:
        copy.wait()
    for d, copy in zip(range(1, owners), trips):
        copy.wait_send()
        there = last_out.at[lax.rem(owner + owners - d, owners)]
        push(there, there, l5.at[d], l6.at[d], twin).wait_recv()


def back(arrays, plan, operands, replies, picks, lasts, call):
    parts, owners = lax.axis_size("mdl"), lax.axis_size("ids")
    half = parts // 2
    slopes, weights, turned, linear, vectors, ratio = operands
    size, hidden = slopes.shape
    inputs = turned.shape[0]
    assert inputs == size
    found_shape = (replies.shape[1], picks.shape[1])
    dma = pltpu.SemaphoreType.DMA
    lines = 2 * hidden // 128
    outs = []
    scratch = [
        pltpu.VMEM(lasts.shape, jnp.float32),
        pltpu.VMEM(lasts.shape[1:], jnp.float32),
        pltpu.VMEM(lasts.shape[1:], jnp.float32),
    ]
    scratch += [dma((parts,))] * 2 + [dma((owners,))] * 4
    scratch += [
        pltpu.VMEM((parts,) + replies.shape, replies.dtype),
        pltpu.VMEM(found_shape, replies.dtype),
    ] + [dma((parts,))] * 4
    scratch += [
        pltpu.VMEM((inputs, hidden), jnp.float32),
        pltpu.VMEM((2, size, BLOCK), jnp.float32),
        dma((2,)),
        pltpu.VMEM((size, BLOCK), jnp.bfloat16),
        pltpu.VMEM((8, hidden), jnp.float32),
        pltpu.VMEM((8, hidden), jnp.float32),
        pltpu.VMEM((parts, lines, 128), jnp.float32),
        pltpu.VMEM((owners, lines, 128), jnp.float32),
        dma((parts,)),
        dma((parts,)),
        dma((owners,)),
        dma((owners,)),
        dma((owners,)),
        dma((owners,)),
    ]
    for rows, lanes, chunks, keep, wire in plan:
        piece = rows // owners
        outs.append(
            jax.ShapeDtypeStruct(
                (owners // 2, 2, piece, lanes) if keep else (lanes, piece), jnp.float32
            )
        )
        scratch += [
            pltpu.VMEM((2, half, rows, lanes // chunks) if keep else (8, 128), jnp.float32),
            pltpu.VMEM((half, rows, lanes), jnp.float32),
            pltpu.VMEM((rows, lanes), wire),
            pltpu.VMEM((rows, lanes), wire),
            pltpu.VMEM((rows, lanes), wire),
            pltpu.VMEM((owners, piece, lanes), wire),
            dma((chunks, half)),
            dma((chunks, half)),
            dma((chunks, half)),
            dma((chunks,)),
            dma((chunks,)),
            dma((chunks, owners)),
            dma((chunks, owners)),
        ]
        if keep:
            scratch += [
                dma((chunks, owners // 2)),
                dma((chunks, owners // 2)),
                dma((chunks,)),
                dma((chunks,)),
            ]
    held = pl.BlockSpec(memory_space=pl.ANY)
    whole = pl.BlockSpec(memory_space=pltpu.VMEM)
    found = pl.pallas_call(
        functools.partial(back_kernel, parts, owners, plan),
        out_shape=tuple(outs)
        + (
            jax.ShapeDtypeStruct((parts,) + found_shape, replies.dtype),
            jax.ShapeDtypeStruct((lines, 128), jnp.float32),
            jax.ShapeDtypeStruct(lasts.shape[1:], jnp.float32),
        ),
        in_specs=[held] * len(arrays) + [whole, whole, whole, held, whole, whole] + [whole] * 3,
        out_specs=(whole,) * (len(plan) + 3),
        scratch_shapes=scratch,
        compiler_params=pltpu.CompilerParams(
            collective_id=call, has_side_effects=True, vmem_limit_bytes=67043328
        ),
        name="back",
    )(*arrays, *operands, replies, picks, lasts)
    grads = tuple(v.reshape(-1, v.shape[-1]) for v in found[: len(plan)])
    return grads + (found[-3], found[-2].reshape(2, hidden), found[-1].reshape(-1, lasts.shape[-1]))


def total(vectors, small, extras, kinds, call):
    rows = [v.reshape(-1, LANES) for v in vectors]
    sizes = [r.shape[0] for r in rows]
    if small is not None:
        rows.append(jnp.pad(small.reshape(1, -1), ((0, 7), (0, LANES - small.size))))
    summed, *moved = exchange(jnp.concatenate(rows, axis=0), extras, kinds, call)
    found, start = [], 0
    for size in sizes:
        found.append(summed[start : start + size].reshape(-1))
        start += size
    if small is not None:
        found.append(summed[start, : small.size])
    return found, moved


def body(
    hash_codes,
    request_ids,
    request_counts,
    token_slots,
    cotangent,
    weight_first,
    weight_second,
    weight_final,
    norm_params,
    bias_final,
    moment_first,
    square_first,
    moment_second,
    square_second,
    moment_final,
    square_final,
    moment_norm,
    square_norm,
    moment_bias,
    square_bias,
):
    owners = lax.axis_size("ids")
    parts = lax.axis_size("mdl")
    part = lax.axis_index("mdl")
    range_rows = hash_codes.shape[0]
    rows = range_rows // parts
    slots_per = request_ids.shape[1]
    piece = slots_per // parts
    out_width = weight_final.shape[1]
    width = weight_first.shape[1]
    wide = width + (-width) % LANES
    hidden = wide * parts
    more = wide - width
    token_count = token_slots.shape[0]
    token_piece = token_count // parts
    token_total = token_count * owners

    encoded = ((hash_codes.astype(jnp.float32) + 0.5) / 512.0 - 1.0).astype(jnp.bfloat16)
    owner_row = jnp.arange(owners, dtype=jnp.int32)[:, None]
    wanted = jnp.where(
        jnp.arange(slots_per, dtype=jnp.int32)[None, :] < request_counts[:, None],
        request_ids - owner_row * range_rows,
        range_rows,
    )
    slot_owner = token_slots // slots_per
    slot_place = token_slots % slots_per - part * piece
    slot_here = jnp.where(
        (slot_place >= 0) & (slot_place < piece), slot_owner * piece + slot_place, -1
    )
    first_low, features, norm_all, final_all, received, slot_sum = front(
        jnp.pad(weight_first.astype(jnp.bfloat16), ((0, 0), (0, more))),
        encoded.reshape(parts, rows, -1),
        jnp.pad(norm_params, ((0, 4), (0, more))),
        jnp.pad(weight_final.astype(jnp.bfloat16).T, ((0, 0), (0, more))),
        wanted.reshape(owners, 1, slots_per),
        slot_here.reshape(1, token_count),
        cotangent.T,
        owners * piece,
        5,
    )
    norm_all = norm_all.transpose(1, 0, 2).reshape(-1, hidden)[:4]
    final_low = final_all.transpose(1, 0, 2).reshape(out_width, hidden)
    second_turned = weight_second.T.astype(jnp.bfloat16)
    second_part = jnp.concatenate(
        [
            jnp.pad(second_turned[:, width * k : width * (k + 1)], ((0, more), (0, more)))
            for k in range(parts)
        ],
        axis=1,
    )
    second_part, first_low = lax.optimization_barrier((second_part, first_low))
    second_low = lax.all_gather(second_part, "mdl", axis=0, tiled=True)

    received = received.reshape(owners, slots_per)
    here = part * rows + jnp.arange(rows, dtype=jnp.int32)
    live_mask = jnp.max(
        (received.reshape(1, -1) == here[:, None]).astype(jnp.float32), axis=1
    )
    slots_mine = lax.dynamic_slice(received, (0, part * piece), (owners, piece)).reshape(-1)
    pick_rows = (
        slots_mine[:, None] == lax.broadcasted_iota(jnp.int32, (owners * piece, range_rows), 1)
    ).astype(jnp.bfloat16)

    sent = jnp.concatenate(split_two(slot_sum / token_total), axis=0)
    sent = sent.reshape(2 * out_width, owners, piece).transpose(1, 0, 2)

    linear_one = jnp.dot(features, first_low, preferred_element_type=jnp.float32)
    active_one = mish(linear_one)
    weighted_one = live_mask[:, None] * active_one
    (*sums_one, live_count), (arrived,) = total(
        [jnp.sum(weighted_one, 0), jnp.sum(weighted_one * active_one, 0)],
        jnp.sum(live_mask).reshape(1),
        [sent],
        (("ids", True),),
        0,
    )
    live_count = live_count[0]
    mean_one = sums_one[0] / live_count
    scale_one = lax.rsqrt(sums_one[1] / live_count - mean_one * mean_one + norm_epsilon)
    unit_one = (active_one - mean_one) * scale_one
    normed_one = (norm_all[0] * unit_one + norm_all[1]).astype(jnp.bfloat16)
    arrived = arrived.transpose(1, 0, 2).reshape(2 * out_width, owners * piece)
    row_part = jnp.dot(arrived, pick_rows, preferred_element_type=jnp.float32)
    row_part = (row_part[:out_width] + row_part[out_width:]).reshape(out_width, parts, rows)
    linear_two = contract(normed_one, second_low, 1, 1)
    active_two = mish(linear_two)
    weighted_two = live_mask[:, None] * active_two
    sums_two, (row_parts,) = total(
        [jnp.sum(weighted_two, 0), jnp.sum(weighted_two * active_two, 0)],
        None,
        [row_part.transpose(1, 0, 2)],
        (("mdl", True),),
        1,
    )
    row_grad = jnp.sum(row_parts, 0)
    mean_two = sums_two[0] / live_count
    scale_two = lax.rsqrt(sums_two[1] / live_count - mean_two * mean_two + norm_epsilon)
    unit_two = (active_two - mean_two) * scale_two
    normed_two = (norm_all[2] * unit_two + norm_all[3]).astype(jnp.bfloat16)
    embedding = contract(final_low, normed_two, 1, 1) + bias_final[:, None]

    grad_embed = (
        row_grad + 2.0 * penalty_weight / live_count * live_mask[None, :] * embedding
    ).astype(jnp.bfloat16)
    incoming_two = contract(grad_embed, final_low, 0, 0)
    (*sums_two, grad_bias), (embed_range,) = total(
        [jnp.sum(incoming_two * unit_two, 0), jnp.sum(incoming_two, 0)],
        jnp.sum(grad_embed.astype(jnp.float32), 1),
        [embedding.astype(jnp.bfloat16)],
        (("mdl", False),),
        2,
    )
    embed_range = embed_range.transpose(1, 0, 2).reshape(out_width, range_rows)
    replies = contract(embed_range, pick_rows, 1, 1).astype(jnp.bfloat16)
    replies = replies.reshape(out_width, owners, piece).transpose(1, 0, 2)
    local_final = contract(grad_embed, normed_two, 1, 0).reshape(out_width, parts, wide)
    local_final = local_final.transpose(1, 0, 2).reshape(parts, owners, out_width // owners, wide)
    outgoing_two = norm_back(
        incoming_two, unit_two, norm_all[2], scale_two, live_mask, sums_two[0], sums_two[1], live_count
    )
    grad_linear_two = (mish_slope(linear_two) * outgoing_two).astype(jnp.bfloat16)
    local_second = contract(grad_linear_two, normed_one, 0, 0).reshape(parts, wide, hidden)
    tokens_mine = lax.dynamic_slice(token_slots, (part * token_piece,), (token_piece,))
    second_sum, first_sum, tokens, sums_one, final_sum = back(
        (local_second,),
        (
            (wide, hidden, 8, True, jnp.bfloat16),
            (features.shape[1], wide, wide // BLOCK, False, jnp.bfloat16),
        ),
        (
            grad_linear_two,
            second_low,
            features.T,
            linear_one,
            jnp.pad(jnp.stack([mean_one, scale_one, norm_all[0]]), ((0, 5), (0, 0))),
            (live_mask / live_count)[:, None],
        ),
        replies,
        tokens_mine.reshape(1, token_piece),
        local_final,
        4,
    )
    token_embed = tokens.transpose(0, 2, 1).reshape(token_count, out_width)
    grad_second = jnp.concatenate(
        [second_sum[:width, wide * k : wide * k + width] for k in range(parts)], axis=1
    ).T
    grad_final = final_sum[:, :width].T
    grad_first = first_sum[:width].T
    start = part * wide
    grad_norm = lax.dynamic_slice(jnp.stack([*sums_one, *sums_two]), (0, start), (4, width))
    momentum_first, variance_first, master_first = adam(
        weight_first, moment_first, square_first, grad_first, rate_matrix, decay_matrix
    )
    momentum_second, variance_second, master_second = adam(
        weight_second, moment_second, square_second, grad_second, rate_matrix, decay_matrix
    )
    momentum_final, variance_final, master_final = adam(
        weight_final, moment_final, square_final, grad_final, rate_matrix, decay_matrix
    )
    momentum_norm, variance_norm, master_norm = adam(
        norm_params, moment_norm, square_norm, grad_norm, rate_norm, 0.0
    )
    momentum_bias, variance_bias, master_bias = adam(
        bias_final, moment_bias, square_bias, grad_bias, rate_bias, 0.0
    )
    return (
        token_embed,
        momentum_first,
        variance_first,
        master_first,
        master_first.astype(jnp.bfloat16),
        momentum_second,
        variance_second,
        master_second,
        master_second.astype(jnp.bfloat16),
        momentum_final,
        variance_final,
        master_final,
        master_final.astype(jnp.bfloat16),
        momentum_norm,
        variance_norm,
        master_norm,
        momentum_bias,
        variance_bias,
        master_bias,
    )


def solution(mesh):
    rows = P("ids", None)
    grid = P("ids", "mdl")
    columns = P(None, "mdl")
    mdl_rows = P("mdl", None)
    return jax.shard_map(
        body,
        mesh=mesh,
        in_specs=(grid, rows, P("ids"), P("ids"), rows, grid, columns, mdl_rows, columns, P())
        + (grid,) * 2
        + (columns,) * 2
        + (mdl_rows,) * 2
        + (columns,) * 2
        + (P(),) * 2,
        out_specs=(rows,)
        + (grid,) * 4
        + (columns,) * 4
        + (mdl_rows,) * 4
        + (columns,) * 3
        + (P(),) * 3,
        check_vma=False,
    )
```

```python
import functools
import jax
import jax.numpy as jnp
from jax import lax
from jax.experimental import pallas as pl
from jax.experimental.pallas import tpu as pltpu
from jax.sharding import PartitionSpec as P

STEP = 10


beta_one = 0.9
beta_two = 0.999
adam_epsilon = 1e-08
norm_epsilon = 1e-05
penalty_weight = 0.25
decay_matrix = 0.01
rate_matrix = 0.05
rate_norm = 0.5
rate_bias = 0.02
LANES = 128


def mish_parts(inputs):
    grown = jnp.exp(jnp.minimum(inputs, 20.0))
    above = grown * (grown + 2.0)
    inverse = 1.0 / (above + 2.0)
    return grown, above * inverse, inverse


def mish(inputs):
    return inputs * mish_parts(inputs)[1]


def mish_slope(inputs):
    grown, gate, inverse = mish_parts(inputs)
    return gate + 4.0 * jnp.minimum(inputs, 20.0) * (grown * inverse) * ((1.0 + grown) * inverse)


def contract(left, right, left_dim, right_dim):
    return lax.dot_general(
        left, right, (((left_dim,), (right_dim,)), ((), ())), preferred_element_type=jnp.float32
    )


def norm_back(upstream, unit_rows, gain_row, scale_row, live_mask, gain_sum, shift_sum, live_count):
    return scale_row * (
        gain_row * upstream
        - live_mask[:, None] * gain_row * (shift_sum + unit_rows * gain_sum) / live_count
    )


def adam(weight, moment, square, gradient, step_rate, shrink):
    momentum = beta_one * moment + (1.0 - beta_one) * gradient
    variance = beta_two * square + (1.0 - beta_two) * gradient * gradient
    moment_hat = momentum / (1.0 - beta_one**STEP)
    square_hat = variance / (1.0 - beta_two**STEP)
    master = weight - step_rate * (
        moment_hat / (jnp.sqrt(square_hat) + adam_epsilon) + shrink * weight
    )
    return (momentum, variance, master)


def split_two(values):
    high = values.astype(jnp.bfloat16)
    low = (values - high.astype(jnp.float32)).astype(jnp.bfloat16)
    return high, low


def one_hot(index, length, first):
    rows = lax.broadcasted_iota(jnp.int32, (length, index.shape[0]), 0) + first
    return (rows == index[None, :]).astype(jnp.bfloat16)


MESH = pl.DeviceIdType.MESH
BLOCK = 256


def greet(peers):
    barrier = pltpu.get_barrier_semaphore()
    for peer in peers:
        pl.semaphore_signal(barrier, inc=1, device_id=peer, device_id_type=MESH)
    pl.semaphore_wait(barrier, len(peers))


def push(source, target, send_sem, recv_sem, peer):
    return pltpu.make_async_remote_copy(
        src_ref=source,
        dst_ref=target,
        send_sem=send_sem,
        recv_sem=recv_sem,
        device_id=peer,
        device_id_type=MESH,
    )


def gap(axis, size, d):
    return {axis: lax.rem(lax.axis_index(axis) + d, size)}


def exchange_kernel(parts, owners, kinds, *refs):
    extras = len(kinds)
    x_ref, given = refs[0], refs[1 : 1 + extras]
    o_ref, taken = refs[1 + extras], refs[2 + extras : 2 + 2 * extras]
    near, far, send_near, recv_near, send_far, recv_far, *sems = refs[2 + 2 * extras :]
    sizes = {"mdl": parts, "ids": owners}
    part = lax.axis_index("mdl")
    owner = lax.axis_index("ids")
    greet([gap("mdl", parts, d) for d in range(1, parts)] + [gap("ids", owners, d) for d in range(1, owners)])
    copies = [
        push(x_ref, near.at[d], send_near.at[d], recv_near.at[d], gap("mdl", parts, d))
        for d in range(1, parts)
    ]
    for copy in copies:
        copy.start()
    others = []
    for n, (axis, spread) in enumerate(kinds):
        me = lax.axis_index(axis)
        for d in range(1, sizes[axis]):
            peer = gap(axis, sizes[axis], d)
            source = given[n].at[peer[axis]] if spread else given[n]
            copy = push(source, taken[n].at[me], sems[2 * n].at[d], sems[2 * n + 1].at[d], peer)
            copy.start()
            others.append(copy)
        taken[n][me] = given[n][me] if spread else given[n][...]
    near[0] = x_ref[...]
    for copy in copies:
        copy.wait()
    total = near[part]
    for k in range(1, parts):
        total = total + near[lax.rem(part + parts - k, parts)]
    far[0] = total
    copies = [
        push(far.at[0], far.at[d], send_far.at[d], recv_far.at[d], gap("ids", owners, d))
        for d in range(1, owners)
    ]
    for copy in copies:
        copy.start()
    for copy in copies:
        copy.wait()
    total = far[owner]
    for k in range(1, owners):
        total = total + far[lax.rem(owner + owners - k, owners)]
    o_ref[...] = total
    for copy in others:
        copy.wait()


def exchange(x, extras, kinds, call):
    parts, owners = lax.axis_size("mdl"), lax.axis_size("ids")
    sizes = {"mdl": parts, "ids": owners}
    dma = pltpu.SemaphoreType.DMA
    whole = pl.BlockSpec(memory_space=pltpu.VMEM)
    outs = [jax.ShapeDtypeStruct(x.shape, jnp.float32)]
    sems = []
    for extra, (axis, spread) in zip(extras, kinds):
        shape = extra.shape if spread else (sizes[axis],) + extra.shape
        outs.append(jax.ShapeDtypeStruct(shape, extra.dtype))
        sems += [dma((sizes[axis],)), dma((sizes[axis],))]
    return pl.pallas_call(
        functools.partial(exchange_kernel, parts, owners, kinds),
        out_shape=tuple(outs),
        in_specs=[whole] * (1 + len(extras)),
        out_specs=(whole,) * len(outs),
        scratch_shapes=[
            pltpu.VMEM((parts,) + x.shape, jnp.float32),
            pltpu.VMEM((owners,) + x.shape, jnp.float32),
            dma((parts,)),
            dma((parts,)),
            dma((owners,)),
            dma((owners,)),
        ]
        + sems,
        compiler_params=pltpu.CompilerParams(collective_id=call, has_side_effects=True),
        name="exchange",
    )(x, *extras)


def front_kernel(
    parts, owners, first, codes, norms, final, wanted, places, pulls,
    weights, feats, norms_all, final_all, received, slot_sums,
    s1, r1, s2, r2, s3, r3, sc, rc, sn, rn, sw, rw, sl, s4, r4, sx, rx,
):
    part = lax.axis_index("mdl")
    owner = lax.axis_index("ids")
    pair = {"mdl": part + 1 - 2 * lax.rem(part, 2)}
    cross_part = lax.rem(part + 2, parts)
    cross = {"mdl": cross_part}
    rows, width = first.shape
    codes_width = codes.shape[2]
    greet([gap("mdl", parts, d) for d in range(1, parts)] + [gap("ids", owners, d) for d in range(1, owners)])

    def spot(who, which):
        return weights.at[
            pl.ds(pl.multiple_of(who * rows, rows), rows),
            pl.ds(pl.multiple_of(which * width, width), width),
        ]

    split = width // 2

    def side(who, which, k):
        return weights.at[
            pl.ds(pl.multiple_of(who * rows, rows), rows),
            pl.ds(pl.multiple_of(which * width + k * split, split), split),
        ]

    early = push(first.at[:, pl.ds(split, split)], side(owner, part, 1), sx.at[0], rx.at[0], cross)
    early.start()
    mine = feats.at[:, pl.ds(pl.multiple_of(part * codes_width, codes_width), codes_width)]
    locals_ = [
        pltpu.make_async_copy(first, spot(owner, part), sl.at[0]),
        pltpu.make_async_copy(codes.at[part], mine, sl.at[1]),
    ]
    for copy in locals_:
        copy.start()
    ones, lines = [], []
    for d in range(1, owners):
        peer = gap("ids", owners, d)
        copy = push(first, spot(owner, part), s1.at[d], r1.at[d], peer)
        copy.start()
        ones.append(copy)
        copy = push(wanted.at[peer["ids"]], received.at[owner], sw.at[d], rw.at[d], peer)
        copy.start()
        lines.append(copy)
    for d in range(1, parts):
        peer = gap("mdl", parts, d)
        for n, (source, target) in enumerate(((norms, norms_all), (final, final_all))):
            copy = push(source, target.at[part], sn.at[n, d], rn.at[n, d], peer)
            copy.start()
            lines.append(copy)
    for d in range(1, parts):
        peer = gap("mdl", parts, d)
        copy = push(codes.at[peer["mdl"]], mine, sc.at[d], rc.at[d], peer)
        copy.start()
        lines.append(copy)
    received[owner] = wanted[owner]
    norms_all[part] = norms[...]
    final_all[part] = final[...]
    early.wait_send()
    lent = side(owner, cross_part, 1)
    push(lent, lent, sx.at[0], rx.at[0], cross).wait_recv()
    fours = [push(lent, lent, s4.at[d], r4.at[d], gap("ids", owners, d)) for d in range(1, owners)]
    for copy in fours:
        copy.start()
    tokens, slots = places.shape[1], slot_sums.shape[1]
    run = min(tokens, 1024)
    runs = tokens // run

    def gather_slots(start, stop):
        def one(n, none):
            at = pl.ds(pl.multiple_of(n * BLOCK, BLOCK), BLOCK)

            def body(k, summed):
                cols = pl.ds(pl.multiple_of(k * run, run), run)
                which = lax.broadcasted_iota(jnp.int32, (BLOCK, run), 0) + n * BLOCK
                here = jnp.where(which == places[0:1, cols], 1.0, 0.0).astype(jnp.bfloat16)
                return summed + contract(pulls[:, cols], here, 1, 1)

            slot_sums[:, at] = lax.fori_loop(
                0, runs, body, jnp.zeros((pulls.shape[0], BLOCK), jnp.float32)
            )
            return none

        lax.fori_loop(start, stop, one, 0)

    count = slots // BLOCK
    gather_slots(0, count // 2)
    twos, threes = [], []
    for d in range(owners):
        who = lax.rem(owner + owners - d, owners)
        if d == 0:
            locals_[0].wait()
        else:
            ones[d - 1].wait_send()
            push(first, spot(who, part), s1.at[d], r1.at[d], pair).wait_recv()
        piece = side(who, part, 0)
        copy = push(piece, piece, s2.at[d], r2.at[d], cross)
        copy.start()
        twos.append(copy)
        piece = spot(who, part)
        copy = push(piece, piece, s3.at[0, d], r3.at[0, d], pair)
        copy.start()
        threes.append(copy)
    gather_slots(count // 2, count)
    for d in range(owners):
        who = lax.rem(owner + owners - d, owners)
        piece = side(who, cross_part, 1)
        if d > 0:
            push(piece, piece, s4.at[d], r4.at[d], pair).wait_recv()
        copy = push(piece, piece, s3.at[2, d], r3.at[2, d], pair)
        copy.start()
        threes.append(copy)
        twos[d].wait_send()
        piece = side(who, cross_part, 0)
        push(piece, piece, s2.at[d], r2.at[d], cross).wait_recv()
        copy = push(piece, piece, s3.at[1, d], r3.at[1, d], pair)
        copy.start()
        threes.append(copy)
    for copy in threes + lines:
        copy.wait()
    for copy in fours:
        copy.wait_send()
    locals_[1].wait()


def front(first, codes, norms, final, wanted, places, pulls, slots, call):
    parts, owners = lax.axis_size("mdl"), lax.axis_size("ids")
    dma = pltpu.SemaphoreType.DMA
    held = pl.BlockSpec(memory_space=pl.ANY)
    whole = pl.BlockSpec(memory_space=pltpu.VMEM)
    shape = jax.ShapeDtypeStruct
    return pl.pallas_call(
        functools.partial(front_kernel, parts, owners),
        out_shape=(
            shape((first.shape[0] * owners, first.shape[1] * parts), first.dtype),
            shape((codes.shape[1], codes.shape[2] * parts), codes.dtype),
            shape((parts,) + norms.shape, norms.dtype),
            shape((parts,) + final.shape, final.dtype),
            shape(wanted.shape, wanted.dtype),
            shape((pulls.shape[0], slots), jnp.float32),
        ),
        in_specs=[whole] * 7,
        out_specs=(held, held, whole, whole, whole, whole),
        scratch_shapes=[dma((owners,))] * 4
        + [dma((3, owners))] * 2
        + [dma((parts,))] * 2
        + [dma((2, parts))] * 2
        + [dma((owners,))] * 2
        + [dma((2,))]
        + [dma((owners,))] * 2
        + [dma((1,))] * 2,
        compiler_params=pltpu.CompilerParams(collective_id=call, has_side_effects=True, vmem_limit_bytes=16 * 1024 * 1024),
        name="front",
    )(first, codes, norms, final, wanted, places, pulls)


def blocks(count, step, body):
    if count == step:
        body(0)
    else:
        @pl.loop(0, count // step)
        def _(k):
            body(pl.multiple_of(k * step, step))


NAMES = (
    "own",
    "got",
    "out_y",
    "in_y",
    "out_f",
    "in_f",
    "s0",
    "r0",
    "sl",
    "sy",
    "ry",
    "sf",
    "rf",
    "sg",
    "rg",
    "st",
    "rt",
)


class Unit:
    pass


def back_kernel(parts, owners, plan, *refs):
    half = parts // 2
    count = len(plan)
    given = refs[: count - 1]
    slopes, weights, turned, linear, vectors, ratio, replies, picks, lasts = refs[count - 1 : count + 8]
    outputs, tokens_out, sums_out = refs[count + 8 : 2 * count + 8], refs[2 * count + 8], refs[2 * count + 9]
    last_out = refs[2 * count + 10]
    scratch = list(refs[2 * count + 11 :])
    last_in, last_sum, last_far, l1, l2, l3, l4, l5, l6 = scratch[:9]
    scratch = scratch[9:]
    gathered, made, sp, rp, st_, rt_ = scratch[:6]
    ra, rb = scratch[18:20]
    held, stream, stream_sem, grown, gains, shifts, near, far, sn, rn, sf_, rf_ = scratch[6:18]
    scratch = scratch[20:]
    inputs = given + (held,)
    part = lax.axis_index("mdl")
    owner = lax.axis_index("ids")
    low, place = lax.rem(part, 2), part // 2
    pair = {"mdl": part + 1 - 2 * low}
    cross = {"mdl": lax.rem(part + 2, parts)}
    side, row = lax.rem(owner, 2), owner // 2
    twin = {"ids": owner + 1 - 2 * side}
    line = owners // 2
    units = []
    for n, (rows, lanes, chunks, keep, wire) in enumerate(plan):
        bufs = {name: scratch.pop(0) for name in NAMES[: 17 if keep else 13]}
        for c in range(chunks):
            u = Unit()
            u.__dict__.update(bufs)
            u.rows, u.lanes, u.width, u.keep, u.c, u.wire = rows, lanes, lanes // chunks, keep, c, wire
            u.piece = rows // owners
            u.cols = pl.ds(c * u.width, u.width)
            u.source, u.out = inputs[n], outputs[n]
            u.here = n == count - 1
            u.after = None
            units.append(u)
    for u, v in zip(units, units[2:]):
        if u.own is v.own and u.own is not None:
            u.after = v
    greet([gap("mdl", parts, d) for d in range(1, parts)] + [gap("ids", owners, d) for d in range(1, owners)])

    def taken(u, k):
        if not u.here:
            return u.source.at[k, :, u.cols]
        start = pl.multiple_of(k * u.lanes + u.c * u.width, u.width)
        return u.source.at[:, pl.ds(start, u.width)]

    def fetch(u):
        u.mine = [
            pltpu.make_async_copy(taken(u, low + 2 * i), u.own.at[u.c % 2, i], u.sl.at[u.c, i])
            for i in range(half)
        ]
        for copy in u.mine:
            copy.start()

    def begin(u):
        u.first = [
            push(
                taken(u, 1 - low + 2 * i),
                u.got.at[i, :, u.cols],
                u.s0.at[u.c, i],
                u.r0.at[u.c, i],
                pair,
            )
            for i in range(half)
        ]
        for copy in u.first:
            copy.start()

    def sweep(u, body):
        step = min(u.rows, 64)
        blocks(u.rows, step, lambda k: body(pl.ds(k, step)))

    def own_part(u, i, at):
        if u.here:
            start = pl.multiple_of((low + 2 * i) * u.lanes + u.c * u.width, u.width)
            return u.source[at, pl.ds(start, u.width)]
        return u.own[u.c % 2, i, at]

    def to_cross(u):
        for copy in u.first + ([] if u.here else u.mine):
            copy.wait()

        def body(at):
            away = own_part(u, 1 - place, at) + u.got[1 - place, at, u.cols]
            u.out_y[at, u.cols] = away.astype(u.wire)
            u.got[place, at, u.cols] = own_part(u, place, at) + u.got[place, at, u.cols]

        sweep(u, body)
        if u.after is not None:
            fetch(u.after)
        u.second = push(
            u.out_y.at[:, u.cols], u.in_y.at[:, u.cols], u.sy.at[u.c], u.ry.at[u.c], cross
        )
        u.second.start()

    def to_owners(u):
        u.second.wait()

        def body(at):
            value = u.got[place, at, u.cols] + u.in_y[at, u.cols].astype(jnp.float32)
            u.got[place, at, u.cols] = value
            u.out_f[at, u.cols] = value.astype(u.wire)

        sweep(u, body)
        u.third = []
        for d in range(1, owners):
            peer = lax.rem(owner + d, owners)
            copy = push(
                u.out_f.at[pl.ds(pl.multiple_of(peer * u.piece, u.piece), u.piece), u.cols],
                u.in_f.at[d, :, u.cols],
                u.sf.at[u.c, d],
                u.rf.at[u.c, d],
                {"ids": peer},
            )
            copy.start()
            u.third.append(copy)

    def finish(u):
        for copy in u.third:
            copy.wait()
        here = pl.ds(pl.multiple_of(owner * u.piece, u.piece), u.piece)
        value = u.got[place, here, u.cols]
        for d in range(1, owners):
            value = value + u.in_f[d, :, u.cols].astype(jnp.float32)
        if not u.keep:
            u.out[u.cols, :] = value.T
            return
        u.out[row, side, :, u.cols] = value
        u.fourth = []
        spot = u.out.at[row, side, :, u.cols]
        for d in range(1, line):
            peer = {"ids": lax.rem(row + d, line) * 2 + side}
            copy = push(spot, spot, u.sg.at[u.c, d], u.rg.at[u.c, d], peer)
            copy.start()
            u.fourth.append(copy)

    def to_twin(u):
        if not u.keep:
            return
        for d, copy in zip(range(1, line), u.fourth):
            copy.wait_send()
            there = u.out.at[lax.rem(row + line - d, line), side, :, u.cols]
            push(there, there, u.sg.at[u.c, d], u.rg.at[u.c, d], twin).wait_recv()
        spot = u.out.at[:, side, :, u.cols]
        u.fifth = push(spot, spot, u.st.at[u.c], u.rt.at[u.c], twin)
        u.fifth.start()

    def close(u):
        if not u.keep:
            return
        u.fifth.wait_send()
        there = u.out.at[:, 1 - side, :, u.cols]
        push(there, there, u.st.at[u.c], u.rt.at[u.c], twin).wait_recv()

    rows, hidden = slopes.shape
    bands = hidden // BLOCK
    step = 64

    def band(k):
        return pl.ds(pl.multiple_of(k * BLOCK, BLOCK), BLOCK)

    def load(k, slot):
        return pltpu.make_async_copy(linear.at[:, band(k)], stream.at[slot], stream_sem.at[slot])

    def unit_rows(values, k):
        mean, scale = vectors[0:1, band(k)], vectors[1:2, band(k)]
        return (mish(values) - mean) * scale

    def incoming(k, slot):
        load(k, slot).wait()

        def multiply(r):
            at = pl.ds(r, rows // 2)
            held[at, band(k)] = jnp.dot(
                slopes[at, :], weights[:, band(k)], preferred_element_type=jnp.float32
            )

        blocks(rows, rows // 2, multiply)

        def body(n, sums):
            at = pl.ds(pl.multiple_of(n * step, step), step)
            value = held[at, band(k)]
            product = value * unit_rows(stream[slot, at, :], k)
            return (
                sums[0] + jnp.sum(product.reshape(step // 8, 8, BLOCK), 0),
                sums[1] + jnp.sum(value.reshape(step // 8, 8, BLOCK), 0),
            )

        zero = jnp.zeros((8, BLOCK), jnp.float32)
        gain, shift = lax.fori_loop(0, rows // step, body, (zero, zero))
        gains[0:1, band(k)] = jnp.sum(gain, 0, keepdims=True)
        shifts[0:1, band(k)] = jnp.sum(shift, 0, keepdims=True)

    def outgoing(k, slot):
        load(k, slot).wait()

        def body(n, none):
            at = pl.ds(pl.multiple_of(n * step, step), step)
            values = stream[slot, at, :]
            scale, gain = vectors[1:2, band(k)], vectors[2:3, band(k)]
            pull = shifts[0:1, band(k)] + unit_rows(values, k) * gains[0:1, band(k)]
            back = scale * (gain * held[at, band(k)] - ratio[at, :] * gain * pull)
            grown[at, :] = (mish_slope(values) * back).astype(jnp.bfloat16)
            return none

        lax.fori_loop(0, rows // step, body, 0)

        def multiply(r):
            at = pl.ds(r, rows // 2)
            held[at, band(k)] = jnp.dot(turned[at, :], grown[...], preferred_element_type=jnp.float32)

        blocks(rows, rows // 2, multiply)

    def bands_of(work, order):
        def body(n, none):
            for slot in range(2):
                k = 2 * n + slot

                @pl.when(k + 1 < bands)
                def _():
                    load(order(k + 1), 1 - slot).start()

                work(order(k), slot)
            return none

        return body

    def exchange_sums(meanwhile):
        lines = hidden // 128
        for n in range(lines):
            at = slice(128 * n, 128 * (n + 1))
            near[0, n : n + 1, :] = gains[0:1, at]
            near[0, lines + n : lines + n + 1, :] = shifts[0:1, at]
        copies = [
            push(near.at[0], near.at[d], sn.at[d], rn.at[d], gap("mdl", parts, d))
            for d in range(1, parts)
        ]
        for copy in copies:
            copy.start()
        meanwhile()
        for copy in copies:
            copy.wait()
        total = near[part]
        for k in range(1, parts):
            total = total + near[lax.rem(part + parts - k, parts)]
        far[0] = total
        copies = [
            push(far.at[0], far.at[d], sf_.at[d], rf_.at[d], gap("ids", owners, d))
            for d in range(1, owners)
        ]
        for copy in copies:
            copy.start()
        for copy in copies:
            copy.wait()
        total = far[owner]
        for k in range(1, owners):
            total = total + far[lax.rem(owner + owners - k, owners)]
        sums_out[...] = total
        for n in range(lines):
            at = slice(128 * n, 128 * (n + 1))
            gains[0:1, at] = total[n : n + 1]
            shifts[0:1, at] = total[lines + n : lines + n + 1]

    def share(source, target, send, recv):
        copies = [
            push(source, target.at[part], send.at[d], recv.at[d], gap("mdl", parts, d))
            for d in range(1, parts)
        ]
        for copy in copies:
            copy.start()
        return copies

    piece = replies.shape[2]
    slots = piece * parts

    def select(q):
        def body(j, summed):
            first = j * slots + q * piece
            place_ = lax.broadcasted_iota(jnp.int32, (piece, picks.shape[1]), 0) + first
            chosen = jnp.where(place_ == picks[...], 1.0, 0.0).astype(jnp.bfloat16)
            return summed + jnp.dot(gathered[q, j], chosen, preferred_element_type=jnp.float32)

        start = jnp.zeros((replies.shape[1], picks.shape[1]), jnp.float32)
        summed = lax.fori_loop(0, owners, body, start)
        made[...] = summed.astype(jnp.bfloat16) if q == 0 else made[...] + summed.astype(jnp.bfloat16)

    asked = []
    for d in range(1, owners):
        peer = gap("ids", owners, d)
        copy = push(replies.at[peer["ids"]], gathered.at[part, owner], ra.at[d], rb.at[d], peer)
        copy.start()
        asked.append(copy)
    gathered[part, owner] = replies[owner]
    last_trips = [
        push(lasts.at[gap("mdl", parts, d)["mdl"]], last_in.at[d], l1.at[d], l2.at[d], gap("mdl", parts, d))
        for d in range(1, parts)
    ]
    for copy in last_trips:
        copy.start()

    def last_to_owners():
        for copy in last_trips:
            copy.wait()
        value = lasts[part]
        for d in range(1, parts):
            value = value + last_in[d]
        last_sum[...] = value
        copies = [
            push(last_sum.at[gap("ids", owners, d)["ids"]], last_far.at[d], l3.at[d], l4.at[d], gap("ids", owners, d))
            for d in range(1, owners)
        ]
        for copy in copies:
            copy.start()
        return copies

    def last_to_all(copies):
        for copy in copies:
            copy.wait()
        value = last_sum[owner]
        for d in range(1, owners):
            value = value + last_far[d]
        last_out[owner] = value
        spot = last_out.at[owner]
        copies = [
            push(spot, spot, l5.at[d], l6.at[d], gap("ids", owners, d)) for d in range(1, owners)
        ]
        for copy in copies:
            copy.start()
        return copies

    whole = [u for u in units if not u.here]
    own = [u for u in units if u.here]
    for u in whole:
        begin(u)
    for n, u in enumerate(whole):
        if n == 0 or u.c < 2:
            fetch(u)
    plain = bands_of(incoming, lambda k: k)
    load(0, 0).start()
    per = bands // parts
    spread = bands_of(outgoing, lambda k: lax.rem(k, parts) * per + k // parts)
    total = len(units)
    stages = (to_cross, to_owners, finish, to_twin, close)
    ready = [0]

    def advance():
        t = ready[0]
        ready[0] += 1
        for s, stage in enumerate(stages):
            if 0 <= t - s < total:
                stage(units[t - s])

    loops = bands // 2
    lax.fori_loop(0, loops // 2, plain, 0)
    advance()
    lax.fori_loop(loops // 2, loops, plain, 0)
    exchange_sums(advance)
    advance()
    for copy in asked:
        copy.wait()
    early = share(gathered.at[part], gathered, sp, rp)
    load(0, 0).start()
    trips = last_to_owners()
    for n in range(loops):
        spread(n, 0)
        if (n + 1) % (loops // per) == 0:
            begin(own[(n + 1) * per // loops - 1])
        advance()
    for copy in early:
        copy.wait()
    trips = last_to_all(trips)
    for q in range(parts):
        advance()
        select(q)
    tokens_out[part] = made[...]
    late = share(made, tokens_out, st_, rt_)
    while ready[0] < total + len(stages) - 1:
        advance()
    for copy in late:
        copy.wait()
    for d, copy in zip(range(1, owners), trips):
        copy.wait_send()
        there = last_out.at[lax.rem(owner + owners - d, owners)]
        push(there, there, l5.at[d], l6.at[d], twin).wait_recv()


def back(arrays, plan, operands, replies, picks, lasts, call):
    parts, owners = lax.axis_size("mdl"), lax.axis_size("ids")
    half = parts // 2
    slopes, weights, turned, linear, vectors, ratio = operands
    size, hidden = slopes.shape
    inputs = turned.shape[0]
    assert inputs == size
    found_shape = (replies.shape[1], picks.shape[1])
    dma = pltpu.SemaphoreType.DMA
    lines = 2 * hidden // 128
    outs = []
    scratch = [
        pltpu.VMEM(lasts.shape, jnp.float32),
        pltpu.VMEM(lasts.shape[1:], jnp.float32),
        pltpu.VMEM(lasts.shape[1:], jnp.float32),
    ]
    scratch += [dma((parts,))] * 2 + [dma((owners,))] * 4
    scratch += [
        pltpu.VMEM((parts,) + replies.shape, replies.dtype),
        pltpu.VMEM(found_shape, replies.dtype),
    ] + [dma((parts,))] * 4
    scratch += [
        pltpu.VMEM((inputs, hidden), jnp.float32),
        pltpu.VMEM((2, size, BLOCK), jnp.float32),
        dma((2,)),
        pltpu.VMEM((size, BLOCK), jnp.bfloat16),
        pltpu.VMEM((8, hidden), jnp.float32),
        pltpu.VMEM((8, hidden), jnp.float32),
        pltpu.VMEM((parts, lines, 128), jnp.float32),
        pltpu.VMEM((owners, lines, 128), jnp.float32),
        dma((parts,)),
        dma((parts,)),
        dma((owners,)),
        dma((owners,)),
        dma((owners,)),
        dma((owners,)),
    ]
    for rows, lanes, chunks, keep, wire in plan:
        piece = rows // owners
        outs.append(
            jax.ShapeDtypeStruct(
                (owners // 2, 2, piece, lanes) if keep else (lanes, piece), jnp.float32
            )
        )
        scratch += [
            pltpu.VMEM((2, half, rows, lanes // chunks) if keep else (8, 128), jnp.float32),
            pltpu.VMEM((half, rows, lanes), jnp.float32),
            pltpu.VMEM((rows, lanes), wire),
            pltpu.VMEM((rows, lanes), wire),
            pltpu.VMEM((rows, lanes), wire),
            pltpu.VMEM((owners, piece, lanes), wire),
            dma((chunks, half)),
            dma((chunks, half)),
            dma((chunks, half)),
            dma((chunks,)),
            dma((chunks,)),
            dma((chunks, owners)),
            dma((chunks, owners)),
        ]
        if keep:
            scratch += [
                dma((chunks, owners // 2)),
                dma((chunks, owners // 2)),
                dma((chunks,)),
                dma((chunks,)),
            ]
    held = pl.BlockSpec(memory_space=pl.ANY)
    whole = pl.BlockSpec(memory_space=pltpu.VMEM)
    found = pl.pallas_call(
        functools.partial(back_kernel, parts, owners, plan),
        out_shape=tuple(outs)
        + (
            jax.ShapeDtypeStruct((parts,) + found_shape, replies.dtype),
            jax.ShapeDtypeStruct((lines, 128), jnp.float32),
            jax.ShapeDtypeStruct(lasts.shape[1:], jnp.float32),
        ),
        in_specs=[held] * len(arrays) + [whole, whole, whole, held, whole, whole] + [whole] * 3,
        out_specs=(whole,) * (len(plan) + 3),
        scratch_shapes=scratch,
        compiler_params=pltpu.CompilerParams(
            collective_id=call, has_side_effects=True, vmem_limit_bytes=67043328
        ),
        name="back",
    )(*arrays, *operands, replies, picks, lasts)
    grads = tuple(v.reshape(-1, v.shape[-1]) for v in found[: len(plan)])
    return grads + (found[-3], found[-2].reshape(2, hidden), found[-1].reshape(-1, lasts.shape[-1]))


def total(vectors, small, extras, kinds, call):
    rows = [v.reshape(-1, LANES) for v in vectors]
    sizes = [r.shape[0] for r in rows]
    if small is not None:
        rows.append(jnp.pad(small.reshape(1, -1), ((0, 7), (0, LANES - small.size))))
    summed, *moved = exchange(jnp.concatenate(rows, axis=0), extras, kinds, call)
    found, start = [], 0
    for size in sizes:
        found.append(summed[start : start + size].reshape(-1))
        start += size
    if small is not None:
        found.append(summed[start, : small.size])
    return found, moved


def body(
    hash_codes,
    request_ids,
    request_counts,
    token_slots,
    cotangent,
    weight_first,
    weight_second,
    weight_final,
    norm_params,
    bias_final,
    moment_first,
    square_first,
    moment_second,
    square_second,
    moment_final,
    square_final,
    moment_norm,
    square_norm,
    moment_bias,
    square_bias,
):
    owners = lax.axis_size("ids")
    parts = lax.axis_size("mdl")
    part = lax.axis_index("mdl")
    range_rows = hash_codes.shape[0]
    rows = range_rows // parts
    slots_per = request_ids.shape[1]
    piece = slots_per // parts
    out_width = weight_final.shape[1]
    width = weight_first.shape[1]
    wide = width + (-width) % LANES
    hidden = wide * parts
    more = wide - width
    token_count = token_slots.shape[0]
    token_piece = token_count // parts
    token_total = token_count * owners

    encoded = ((hash_codes.astype(jnp.float32) + 0.5) / 512.0 - 1.0).astype(jnp.bfloat16)
    owner_row = jnp.arange(owners, dtype=jnp.int32)[:, None]
    wanted = jnp.where(
        jnp.arange(slots_per, dtype=jnp.int32)[None, :] < request_counts[:, None],
        request_ids - owner_row * range_rows,
        range_rows,
    )
    slot_owner = token_slots // slots_per
    slot_place = token_slots % slots_per - part * piece
    slot_here = jnp.where(
        (slot_place >= 0) & (slot_place < piece), slot_owner * piece + slot_place, -1
    )
    first_low, features, norm_all, final_all, received, slot_sum = front(
        jnp.pad(weight_first.astype(jnp.bfloat16), ((0, 0), (0, more))),
        encoded.reshape(parts, rows, -1),
        jnp.pad(norm_params, ((0, 4), (0, more))),
        jnp.pad(weight_final.astype(jnp.bfloat16).T, ((0, 0), (0, more))),
        wanted.reshape(owners, 1, slots_per),
        slot_here.reshape(1, token_count),
        cotangent.T,
        owners * piece,
        5,
    )
    norm_all = norm_all.transpose(1, 0, 2).reshape(-1, hidden)[:4]
    final_low = final_all.transpose(1, 0, 2).reshape(out_width, hidden)
    second_turned = weight_second.T.astype(jnp.bfloat16)
    second_part = jnp.concatenate(
        [
            jnp.pad(second_turned[:, width * k : width * (k + 1)], ((0, more), (0, more)))
            for k in range(parts)
        ],
        axis=1,
    )
    second_part, first_low = lax.optimization_barrier((second_part, first_low))
    second_low = lax.all_gather(second_part, "mdl", axis=0, tiled=True)

    received = received.reshape(owners, slots_per)
    here = part * rows + jnp.arange(rows, dtype=jnp.int32)
    live_mask = jnp.max(
        (received.reshape(1, -1) == here[:, None]).astype(jnp.float32), axis=1
    )
    slots_mine = lax.dynamic_slice(received, (0, part * piece), (owners, piece)).reshape(-1)
    pick_rows = (
        slots_mine[:, None] == lax.broadcasted_iota(jnp.int32, (owners * piece, range_rows), 1)
    ).astype(jnp.bfloat16)

    sent = jnp.concatenate(split_two(slot_sum / token_total), axis=0)
    sent = sent.reshape(2 * out_width, owners, piece).transpose(1, 0, 2)

    linear_one = jnp.dot(features, first_low, preferred_element_type=jnp.float32)
    active_one = mish(linear_one)
    weighted_one = live_mask[:, None] * active_one
    (*sums_one, live_count), (arrived,) = total(
        [jnp.sum(weighted_one, 0), jnp.sum(weighted_one * active_one, 0)],
        jnp.sum(live_mask).reshape(1),
        [sent],
        (("ids", True),),
        0,
    )
    live_count = live_count[0]
    mean_one = sums_one[0] / live_count
    scale_one = lax.rsqrt(sums_one[1] / live_count - mean_one * mean_one + norm_epsilon)
    unit_one = (active_one - mean_one) * scale_one
    normed_one = (norm_all[0] * unit_one + norm_all[1]).astype(jnp.bfloat16)
    arrived = arrived.transpose(1, 0, 2).reshape(2 * out_width, owners * piece)
    row_part = jnp.dot(arrived, pick_rows, preferred_element_type=jnp.float32)
    row_part = (row_part[:out_width] + row_part[out_width:]).reshape(out_width, parts, rows)
    linear_two = contract(normed_one, second_low, 1, 1)
    active_two = mish(linear_two)
    weighted_two = live_mask[:, None] * active_two
    sums_two, (row_parts,) = total(
        [jnp.sum(weighted_two, 0), jnp.sum(weighted_two * active_two, 0)],
        None,
        [row_part.transpose(1, 0, 2)],
        (("mdl", True),),
        1,
    )
    row_grad = jnp.sum(row_parts, 0)
    mean_two = sums_two[0] / live_count
    scale_two = lax.rsqrt(sums_two[1] / live_count - mean_two * mean_two + norm_epsilon)
    unit_two = (active_two - mean_two) * scale_two
    normed_two = (norm_all[2] * unit_two + norm_all[3]).astype(jnp.bfloat16)
    embedding = contract(final_low, normed_two, 1, 1) + bias_final[:, None]

    grad_embed = (
        row_grad + 2.0 * penalty_weight / live_count * live_mask[None, :] * embedding
    ).astype(jnp.bfloat16)
    incoming_two = contract(grad_embed, final_low, 0, 0)
    (*sums_two, grad_bias), (embed_range,) = total(
        [jnp.sum(incoming_two * unit_two, 0), jnp.sum(incoming_two, 0)],
        jnp.sum(grad_embed.astype(jnp.float32), 1),
        [embedding.astype(jnp.bfloat16)],
        (("mdl", False),),
        2,
    )
    embed_range = embed_range.transpose(1, 0, 2).reshape(out_width, range_rows)
    replies = contract(embed_range, pick_rows, 1, 1).astype(jnp.bfloat16)
    replies = replies.reshape(out_width, owners, piece).transpose(1, 0, 2)
    local_final = contract(grad_embed, normed_two, 1, 0).reshape(out_width, parts, wide)
    local_final = local_final.transpose(1, 0, 2).reshape(parts, owners, out_width // owners, wide)
    outgoing_two = norm_back(
        incoming_two, unit_two, norm_all[2], scale_two, live_mask, sums_two[0], sums_two[1], live_count
    )
    grad_linear_two = (mish_slope(linear_two) * outgoing_two).astype(jnp.bfloat16)
    local_second = contract(grad_linear_two, normed_one, 0, 0).reshape(parts, wide, hidden)
    tokens_mine = lax.dynamic_slice(token_slots, (part * token_piece,), (token_piece,))
    second_sum, first_sum, tokens, sums_one, final_sum = back(
        (local_second,),
        (
            (wide, hidden, 8, True, jnp.bfloat16),
            (features.shape[1], wide, wide // BLOCK, False, jnp.bfloat16),
        ),
        (
            grad_linear_two,
            second_low,
            features.T,
            linear_one,
            jnp.pad(jnp.stack([mean_one, scale_one, norm_all[0]]), ((0, 5), (0, 0))),
            (live_mask / live_count)[:, None],
        ),
        replies,
        tokens_mine.reshape(1, token_piece),
        local_final,
        4,
    )
    token_embed = tokens.transpose(0, 2, 1).reshape(token_count, out_width)
    grad_second = jnp.concatenate(
        [second_sum[:width, wide * k : wide * k + width] for k in range(parts)], axis=1
    ).T
    grad_final = final_sum[:, :width].T
    grad_first = first_sum[:width].T
    start = part * wide
    grad_norm = lax.dynamic_slice(jnp.stack([*sums_one, *sums_two]), (0, start), (4, width))
    momentum_first, variance_first, master_first = adam(
        weight_first, moment_first, square_first, grad_first, rate_matrix, decay_matrix
    )
    momentum_second, variance_second, master_second = adam(
        weight_second, moment_second, square_second, grad_second, rate_matrix, decay_matrix
    )
    momentum_final, variance_final, master_final = adam(
        weight_final, moment_final, square_final, grad_final, rate_matrix, decay_matrix
    )
    momentum_norm, variance_norm, master_norm = adam(
        norm_params, moment_norm, square_norm, grad_norm, rate_norm, 0.0
    )
    momentum_bias, variance_bias, master_bias = adam(
        bias_final, moment_bias, square_bias, grad_bias, rate_bias, 0.0
    )
    return (
        token_embed,
        momentum_first,
        variance_first,
        master_first,
        master_first.astype(jnp.bfloat16),
        momentum_second,
        variance_second,
        master_second,
        master_second.astype(jnp.bfloat16),
        momentum_final,
        variance_final,
        master_final,
        master_final.astype(jnp.bfloat16),
        momentum_norm,
        variance_norm,
        master_norm,
        momentum_bias,
        variance_bias,
        master_bias,
    )


def solution(mesh):
    rows = P("ids", None)
    grid = P("ids", "mdl")
    columns = P(None, "mdl")
    mdl_rows = P("mdl", None)
    return jax.shard_map(
        body,
        mesh=mesh,
        in_specs=(grid, rows, P("ids"), P("ids"), rows, grid, columns, mdl_rows, columns, P())
        + (grid,) * 2
        + (columns,) * 2
        + (mdl_rows,) * 2
        + (columns,) * 2
        + (P(),) * 2,
        out_specs=(rows,)
        + (grid,) * 4
        + (columns,) * 4
        + (mdl_rows,) * 4
        + (columns,) * 3
        + (P(),) * 3,
        check_vma=False,
    )
```
